256 devices in a mesh: row: 32 (over z, y), col: 8 (over x, core).
Axes of the slice: x: 4, y: 4, z: 8, core: 2. Of those that a mesh axis runs over, the one named last changes fastest.
Arguments:
- expression: bfloat16 [32768, 1024], P(('row', 'col')), as said below
- power_order: int32 [20], replicated, may hold values from 0 to 19, each once
Outputs:
- log_conn: float32 [32768, 20], P(('row', 'col'))
- fit: float32 [20], replicated
- slope: float32 [20], replicated
The draws below stay inside these ranges and needn't reach their ends.
Inputs may be any that keep to these rules, and one draw needn't show every extreme that they name: `expression`: each gene's row has mean zero and unit variance over the samples, up to rounding.
All inputs are finite; a program needn't handle non-finite values.
Results may differ from the reference program's by a relative error of at most 0.0029.
Values may be sent and summed in bfloat16 or wider, within the bound.
A program may use at most 64 MiB of HBM per device.

```python
import math
import jax
import jax.numpy as jnp
from jax import lax

SAMPLES = 1024
POWERS = 20
BINS = 128
GENES_DEV = 128
GENES = 32768
N_COL = 8


module_count = 192


sub_count = 4


factor_count = 96


def draw_expression(key, part):
    keys = jax.random.split(jax.random.fold_in(key, 11), 9)
    eigen = jax.random.normal(keys[0], (module_count, SAMPLES), jnp.float32)
    sub_eigen = jax.random.normal(keys[1], (module_count * sub_count, SAMPLES), jnp.float32)
    factors = jax.random.normal(keys[2], (factor_count, SAMPLES), jnp.float32)
    choices_three = jax.random.randint(keys[3], (GENES, 3), 0, module_count)
    member = jnp.min(choices_three, axis=1)
    sub_member = member * sub_count + jax.random.randint(keys[4], (GENES,), 0, sub_count)
    module_load = jax.random.uniform(keys[5], (GENES,), jnp.float32, 0.1, 0.8)
    sub_load = jax.random.uniform(keys[6], (GENES,), jnp.float32, 0.1, 0.6)
    loadings = 0.07 * jax.random.normal(keys[7], (GENES, factor_count), jnp.float32)
    noise_weight = jax.random.uniform(keys[8], (GENES,), jnp.float32, 0.4, 1.0)
    noise = jax.random.normal(jax.random.fold_in(keys[8], 3), (GENES, SAMPLES), jnp.float32)
    raw = module_load[:, None] * eigen[member] + sub_load[:, None] * sub_eigen[sub_member]
    raw = raw + jnp.dot(loadings, factors, precision=lax.Precision.HIGHEST) + noise_weight[:, None] * noise
    centered = raw - jnp.mean(raw, axis=1, keepdims=True)
    spread = jnp.sqrt(jnp.mean(centered * centered, axis=1, keepdims=True))
    return (centered / spread).astype(jnp.bfloat16)


def setup_inputs(seed: int = 0) -> dict:
    seeds = jax.random.split(jax.random.key(seed), 3)
    return {
        "expression": draw_expression(jax.random.fold_in(seeds[2], 71), 0),
        "power_order": jax.random.permutation(seeds[1], POWERS).astype(jnp.int32),
    }


def power_sums(rows, partners):
    corr = lax.dot_general(rows, partners, (((1,), (1,)), ((), ())), preferred_element_type=jnp.float32) / SAMPLES
    magnitude = jnp.abs(corr)
    current = magnitude
    sums = []
    for power in range(POWERS):
        sums.append(jnp.sum(current, axis=1))
        current = current * magnitude
    return jnp.stack(sums, axis=1)


def scale_free_fit(hist, log_total):
    centers = jnp.arange(BINS, dtype=jnp.float32) * (log_total / (BINS - 1))
    weight_sum = jnp.sum(hist, axis=1, keepdims=True)
    ylog = jnp.log(hist + 1.0) - log_total
    xmean = jnp.sum(hist * centers[None, :], axis=1, keepdims=True) / weight_sum
    ymean = jnp.sum(hist * ylog, axis=1, keepdims=True) / weight_sum
    xdev = centers[None, :] - xmean
    ydev = ylog - ymean
    sxx = jnp.maximum(jnp.sum(hist * xdev * xdev, axis=1) / weight_sum[:, 0], 0.05)
    syy = jnp.maximum(jnp.sum(hist * ydev * ydev, axis=1) / weight_sum[:, 0], 0.05)
    sxy = jnp.sum(hist * xdev * ydev, axis=1) / weight_sum[:, 0]
    return -sxy * jnp.abs(sxy) / (sxx * syy), sxy / sxx


def soft_hist(log_conn, log_total):
    pos = log_conn * ((BINS - 1) / log_total)
    levels = jnp.arange(BINS, dtype=jnp.float32)
    weights = jnp.maximum(0.0, 1.0 - jnp.abs(pos[:, :, None] - levels[None, None, :]))
    return jnp.sum(weights, axis=0)


def reference(expression, power_order):
    block = GENES_DEV * N_COL
    count = GENES // block
    blocks = expression.reshape(count, block, SAMPLES)
    conn = lax.map(lambda rows: power_sums(rows, expression), blocks).reshape(GENES, POWERS)
    selector = (power_order[:, None] == jnp.arange(POWERS, dtype=jnp.int32)[None, :]).astype(jnp.float32)
    picked = jnp.dot(conn, selector.T, precision=lax.Precision.HIGHEST)
    log_conn = jnp.log(picked)
    log_total = math.log(GENES)
    hist = soft_hist(log_conn, log_total)
    fit, slope = scale_free_fit(hist, log_total)
    return log_conn, fit, slope
```

```python
import functools
import math

import jax
import jax.numpy as jnp
from jax import lax
from jax.experimental import pallas as pl
from jax.experimental.pallas import tpu as pltpu
from jax.sharding import Mesh
from jax.sharding import PartitionSpec as P

AXES = ("row_0", "row_1", "col_0", "col_1")
POWERS = 20
BINS = 128
LANES = 128
SLABS = 8
PIECE = 64
CHUNK = 256
STEPS = 8
MESH_ID = pl.DeviceIdType.MESH


def wrap4(d):
    return {0: 0, 1: 1, 2: 2, 3: -1}[d % 4]


X_UP = [(1, 0, 0), (1, 0, 1), (2, 0, 0), (1, 1, 1), (1, -1, 1), (2, 0, 1), (1, 2, 1)]
X_DOWN = [(-1, 0, 0), (-1, 0, 1), (-1, 1, 1), (-1, -1, 1), (-1, 2, 1), (2, 1, 1), (2, -1, 1), (2, 2, 1)]


def mirrored(order):
    return [(dy, dx, 1 - half) for dx, dy, half in order]


ARRIVALS = {
    (1, 0): X_UP,
    (-1, 0): X_DOWN,
    (0, 1): mirrored(X_UP),
    (0, -1): mirrored(X_DOWN),
}
LINKS = list(ARRIVALS)


def place_pieces():
    row, step_of = {}, {(0, 0, 0): 0, (0, 0, 1): 0}
    for step in range(1, STEPS + 1):
        free = {0: [0, 2], 1: [1, 3]}
        here = [order[step - 1] for order in ARRIVALS.values() if step <= len(order)]
        if step == STEPS:
            here = [(0, 0, 0), (0, 0, 1)] + here
        for piece in here:
            slot = free[piece[2]].pop(0)
            row[piece] = (step - 1) * CHUNK + slot * PIECE
            step_of.setdefault(piece, step)
    return row, step_of


ROW, STEP_OF = place_pieces()


def sends_by_step():
    out = [[] for _ in range(STEPS + 1)]
    for k, (lx, ly) in enumerate(LINKS):
        for i, (dx, dy, half) in enumerate(ARRIVALS[(lx, ly)]):
            mine = (wrap4(dx - lx), wrap4(dy - ly), half)
            out[STEP_OF[mine]].append((k, i, ROW[mine], ROW[(dx, dy, half)]))
    return out


PLANE_SENDS = sends_by_step()
PEERS = [(dx, dy) for dx in (0, 1, -1, 2) for dy in (0, 1, -1, 2) if (dx, dy) != (0, 0)]
Z_STEPS = 7
B_BLOCKS = [(0, 768), (768, 512), (1280, 512), (1792, 256)]


def tree_sum(values):
    while len(values) > 1:
        pairs = [a + b for a, b in zip(values[::2], values[1::2])]
        values = pairs + ([values[-1]] if len(values) % 2 else [])
    return values[0]


def kernel(
    log_total,
    samples,
    x_ref,
    order_ref,
    log_conn_ref,
    fit_ref,
    slope_ref,
    genes,
    partners,
    acc,
    tile,
    self_ref,
    outgoing,
    incoming,
    conn_ref,
    hist_ref,
    plane_ref,
    plane_hist,
    line_hist,
    local_sem,
    plane_send,
    plane_recv,
    z_send,
    z_recv,
    core_send,
    core_recv,
    part_send,
    part_recv,
    hist_send,
    hist_recv,
    line_send,
    line_recv,
):
    z, y, x, core = (lax.axis_index(a) for a in AXES)

    def at(dx=0, dy=0, dz=0, dc=0):
        return (
            lax.rem(z + (dz + 8), 8),
            lax.rem(y + (dy + 4), 4),
            lax.rem(x + (dx + 4), 4),
            lax.rem(core + dc, 2),
        )

    own_row = ROW[(0, 0, 0)]
    loads = []
    for k in range(SLABS):
        cols = pl.ds(k * LANES, LANES)
        loads.append(
            pltpu.make_async_copy(
                x_ref.at[:, cols], genes.at[k, pl.ds(own_row, 2 * PIECE), :], local_sem.at[0, k]
            )
        )
        loads.append(
            pltpu.make_async_copy(
                x_ref.at[:, cols], partners.at[k, pl.ds(0, 2 * PIECE), :], local_sem.at[1, k]
            )
        )
    for copy in loads:
        copy.start()

    barrier = pltpu.get_barrier_semaphore()
    near = [at(dx=1), at(dx=-1), at(dy=1), at(dy=-1), at(dz=1), at(dz=-1), at(dc=1)]
    for device in near:
        pl.semaphore_signal(barrier, inc=1, device_id=device, device_id_type=MESH_ID)
    acc[...] = jnp.zeros_like(acc)
    for copy in loads:
        copy.wait()
    pl.semaphore_wait(barrier, len(near))

    sent = []

    def remote(src, dst, send_sem, recv_sem, device):
        return pltpu.make_async_remote_copy(
            src_ref=src,
            dst_ref=dst,
            send_sem=send_sem,
            recv_sem=recv_sem,
            device_id=device,
            device_id_type=MESH_ID,
        )

    def plane_copy(k, i, src, dst):
        lx, ly = LINKS[k]
        return remote(
            genes.at[:, pl.ds(src, PIECE), :],
            genes.at[:, pl.ds(dst, PIECE), :],
            plane_send.at[k, i],
            plane_recv.at[k, i],
            at(dx=-lx, dy=-ly),
        )

    def z_row(direction, step):
        return step * CHUNK + (0 if direction == 1 else PIECE)

    def z_copy(direction, step):
        if step <= 2:
            first = step == 1
            src = 0 if first == (direction == 1) else PIECE
        else:
            src = z_row(direction, step - 2)
        side = 0 if direction == 1 else 1
        return remote(
            partners.at[:, pl.ds(src, PIECE), :],
            partners.at[:, pl.ds(z_row(direction, step), PIECE), :],
            z_send.at[side, step - 1],
            z_recv.at[side, step - 1],
            at(dz=-direction),
        )

    def core_copy(step):
        return remote(
            partners.at[:, pl.ds(step * CHUNK, 2 * PIECE), :],
            partners.at[:, pl.ds(step * CHUNK + 2 * PIECE, 2 * PIECE), :],
            core_send.at[step],
            core_recv.at[step],
            at(dc=1),
        )

    def start(copy):
        copy.start()
        sent.append(copy)

    def communicate(step):
        if step:
            for k, link in enumerate(LINKS):
                if step <= len(ARRIVALS[link]):
                    plane_copy(k, step - 1, 0, ROW[ARRIVALS[link][step - 1]]).wait_recv()
            if step <= Z_STEPS:
                for direction in (1, -1):
                    z_copy(direction, step).wait_recv()
        for send in PLANE_SENDS[step]:
            start(plane_copy(*send))
        for later in (1, 2) if step == 0 else (step + 2,):
            if later <= Z_STEPS:
                for direction in (1, -1):
                    start(z_copy(direction, later))
        if step <= Z_STEPS:
            start(core_copy(step))

    def partner_rows_ready(step):
        core_copy(step).wait_recv()

    def lanes_of(ref, first, count):
        return jnp.concatenate(
            [ref[k, pl.ds(pl.multiple_of(first, PIECE), count), :] for k in range(SLABS)], axis=1
        )

    scale = 1.0 / samples

    def work(chunk, first, rows):
        base = pl.multiple_of(chunk * CHUNK, CHUNK)
        tile[pl.ds(0, rows), :] = lax.dot_general(
            lanes_of(partners, first, rows),
            lanes_of(genes, base, CHUNK),
            (((1,), (1,)), ((), ())),
            preferred_element_type=jnp.float32,
        )
        if first == 0:

            @pl.when(chunk == STEPS - 1)
            def _():
                block = tile[pl.ds(0, 2 * PIECE), pl.ds(0, 2 * PIECE)]
                same = lax.broadcasted_iota(jnp.int32, block.shape, 0) == lax.broadcasted_iota(
                    jnp.int32, block.shape, 1
                )
                own = jnp.sum(jnp.where(same, block, 0.0), axis=0, keepdims=True)
                self_ref[...] = jnp.abs(own) * scale
                tile[pl.ds(0, 2 * PIECE), pl.ds(0, 2 * PIECE)] = jnp.where(same, 0.0, block)

        for i in range(rows // 256):
            for j in range(CHUNK // LANES):
                magnitude = [
                    jnp.abs(
                        tile[pl.ds(i * 256 + q * 16, 16), pl.ds(j * LANES, LANES)].astype(
                            jnp.bfloat16
                        )
                        * scale
                    )
                    for q in range(16)
                ]
                current = magnitude
                for power in range(POWERS):
                    total = tree_sum(current).astype(jnp.float32)
                    acc[power, :, pl.ds(base + j * LANES, LANES)] += total[0:8] + total[8:16]
                    if power < POWERS - 1:
                        current = [a * b for a, b in zip(current, magnitude)]

    def work_over(chunks, block):
        first, rows = B_BLOCKS[block]

        def body(chunk, carry):
            work(chunk, first, rows)
            return carry

        lax.fori_loop(chunks[0], chunks[1], body, 0)

    communicate(0)
    for phase in range(4):
        for step in (2 * phase + 1, 2 * phase + 2):
            communicate(step)
        for step in [0, 1, 2] if phase == 0 else [2 * phase + 1, 2 * phase + 2]:
            if step <= Z_STEPS:
                partner_rows_ready(step)
        for block in range(phase):
            work_over((2 * phase, 2 * phase + 2), block)
        work_over((0, 2 * phase + 2), phase)

    sums = jnp.sum(acc[...], axis=1)
    low_half = lax.broadcasted_iota(jnp.int32, (POWERS, LANES), 1) < PIECE

    def sums_of(dx, dy):
        low, high = (ROW[(dx, dy, half)] // LANES * LANES for half in (0, 1))
        return jnp.where(low_half, sums[:, low : low + LANES], sums[:, high : high + LANES])

    for n, (dx, dy) in enumerate(PEERS):
        outgoing[n, pl.ds(0, POWERS), :] = sums_of(dx, dy)
        outgoing[n, pl.ds(POWERS, 4), :] = jnp.zeros((4, LANES), jnp.float32)

    def part_copy(n):
        dx, dy = PEERS[n]
        return remote(
            outgoing.at[n], incoming.at[n], part_send.at[n], part_recv.at[n], at(dx=dx, dy=dy)
        )

    for n in range(len(PEERS)):
        start(part_copy(n))
    total = sums_of(0, 0)
    own = self_ref[...]
    powers = [own]
    for _ in range(POWERS - 1):
        powers.append(powers[-1] * own)
    total = total + jnp.concatenate(powers, axis=0)
    for n in range(len(PEERS)):
        part_copy(n).wait_recv()
        total = total + incoming[n, pl.ds(0, POWERS), :]
    conn_ref[pl.ds(0, POWERS), :] = total
    picked = jnp.concatenate([conn_ref[pl.ds(order_ref[t], 1), :] for t in range(POWERS)], axis=0)
    log_conn = jnp.log(picked)
    log_conn_ref[...] = log_conn

    position = log_conn * ((BINS - 1) / log_total)
    position = jnp.concatenate(
        [position, jnp.zeros((LANES - POWERS, LANES), jnp.float32)], axis=0
    ).T
    levels = lax.broadcasted_iota(jnp.int32, (LANES, BINS), 1).astype(jnp.float32)
    for t in range(POWERS):
        weights = jnp.maximum(0.0, 1.0 - jnp.abs(position[:, t : t + 1] - levels))
        hist_ref[pl.ds(t, 1), :] = jnp.sum(weights, axis=0, keepdims=True)
    hist_ref[pl.ds(POWERS, 4), :] = jnp.zeros((4, BINS), jnp.float32)

    here = x * 4 + y

    def hist_copy(n, src):
        dx, dy = PEERS[n]
        return remote(
            hist_ref, plane_hist.at[src], hist_send.at[n], hist_recv.at[n], at(dx=dx, dy=dy)
        )

    for n in range(len(PEERS)):
        start(hist_copy(n, here))
    plane_hist[here] = hist_ref[...]
    for n in range(len(PEERS)):
        dx, dy = PEERS[n]
        hist_copy(n, lax.rem(x + (4 - dx), 4) * 4 + lax.rem(y + (4 - dy), 4)).wait_recv()
    plane_ref[...] = tree_sum([plane_hist[i] for i in range(16)])

    line = z * 2 + core
    line_peers = [(dz, dc) for dz in range(8) for dc in range(2) if (dz, dc) != (0, 0)]

    def line_copy(n, src):
        dz, dc = line_peers[n]
        return remote(
            plane_ref, line_hist.at[src], line_send.at[n], line_recv.at[n], at(dz=dz, dc=dc)
        )

    for n in range(len(line_peers)):
        start(line_copy(n, line))
    line_hist[line] = plane_ref[...]
    for n in range(len(line_peers)):
        dz, dc = line_peers[n]
        line_copy(n, lax.rem(z + (8 - dz), 8) * 2 + lax.rem(core + dc, 2)).wait_recv()
    hist = tree_sum([line_hist[i] for i in range(16)])

    hist = jnp.concatenate([hist, jnp.zeros((LANES - 24, BINS), jnp.float32)], axis=0).T
    centers = lax.broadcasted_iota(jnp.int32, hist.shape, 0).astype(jnp.float32) * (
        log_total / (BINS - 1)
    )

    def over_bins(value):
        return jnp.sum(value, axis=0, keepdims=True)

    weight_sum = over_bins(hist)
    ylog = jnp.log(hist + 1.0) - log_total
    xdev = centers - over_bins(hist * centers) / weight_sum
    ydev = ylog - over_bins(hist * ylog) / weight_sum
    sxx = jnp.maximum(over_bins(hist * xdev * xdev) / weight_sum, 0.05)
    syy = jnp.maximum(over_bins(hist * ydev * ydev) / weight_sum, 0.05)
    sxy = over_bins(hist * xdev * ydev) / weight_sum
    fit_ref[...] = (-sxy * jnp.abs(sxy) / (sxx * syy))[:, :POWERS]
    slope_ref[...] = (sxy / sxx)[:, :POWERS]

    for copy in sent:
        copy.wait_send()


def on_device(expression, power_order):
    genes_dev, samples = expression.shape
    powers = power_order.shape[0]
    total_genes = genes_dev * lax.axis_size(AXES)
    plane, line = len(PEERS), 15
    dma = pltpu.SemaphoreType.DMA
    log_conn, fit, slope = pl.pallas_call(
        functools.partial(kernel, math.log(total_genes), samples),
        out_shape=(
            jax.ShapeDtypeStruct((powers, genes_dev), jnp.float32),
            jax.ShapeDtypeStruct((1, powers), jnp.float32),
            jax.ShapeDtypeStruct((1, powers), jnp.float32),
        ),
        in_specs=[pl.BlockSpec(memory_space=pl.ANY), pl.BlockSpec(memory_space=pltpu.SMEM)],
        out_specs=(pl.BlockSpec(memory_space=pltpu.VMEM),) * 3,
        scratch_shapes=[
            pltpu.VMEM((SLABS, 2048, LANES), jnp.bfloat16),
            pltpu.VMEM((SLABS, 2048, LANES), jnp.bfloat16),
            pltpu.VMEM((POWERS, 8, 2048), jnp.float32),
            pltpu.VMEM((768, CHUNK), jnp.float32),
            pltpu.VMEM((1, LANES), jnp.float32),
            pltpu.VMEM((plane, 24, LANES), jnp.float32),
            pltpu.VMEM((plane, 24, LANES), jnp.float32),
            pltpu.VMEM((24, LANES), jnp.float32),
            pltpu.VMEM((24, BINS), jnp.float32),
            pltpu.VMEM((24, BINS), jnp.float32),
            pltpu.VMEM((16, 24, BINS), jnp.float32),
            pltpu.VMEM((16, 24, BINS), jnp.float32),
            dma((2, SLABS)),
            dma((4, STEPS)),
            dma((4, STEPS)),
            dma((2, Z_STEPS)),
            dma((2, Z_STEPS)),
            dma((STEPS,)),
            dma((STEPS,)),
            dma((plane,)),
            dma((plane,)),
            dma((plane,)),
            dma((plane,)),
            dma((line,)),
            dma((line,)),
        ],
        compiler_params=pltpu.CompilerParams(
            collective_id=0, has_side_effects=True, vmem_limit_bytes=48 * 1024 * 1024
        ),
        name="coexpression",
    )(expression, power_order)
    return log_conn.T, fit.reshape(powers), slope.reshape(powers)


def solution(mesh):
    torus = Mesh(mesh.devices.reshape(8, 4, 4, 2), AXES)
    along = P(AXES, None)
    return jax.shard_map(
        on_device,
        mesh=torus,
        in_specs=(along, P()),
        out_specs=(along, P(), P()),
        check_vma=False,
    )
```

```python
import functools
import math

import jax
import jax.numpy as jnp
from jax import lax
from jax.experimental import pallas as pl
from jax.experimental.pallas import tpu as pltpu
from jax.sharding import Mesh
from jax.sharding import PartitionSpec as P

AXES = ("row_0", "row_1", "col_0", "col_1")
POWERS = 20
BINS = 128
LANES = 128
SLABS = 8
PIECE = 64
CHUNK = 256
STEPS = 8
TOKEN_POWER = 16
MESH_ID = pl.DeviceIdType.MESH


def wrap4(d):
    return {0: 0, 1: 1, 2: 2, 3: -1}[d % 4]


X_UP = [(1, 0, 0), (1, 0, 1), (2, 0, 0), (1, 1, 1), (1, -1, 1), (2, 0, 1), (1, 2, 1)]
X_DOWN = [(-1, 0, 0), (-1, 0, 1), (-1, 1, 1), (-1, -1, 1), (-1, 2, 1), (2, 1, 1), (2, -1, 1), (2, 2, 1)]


def mirrored(order):
    return [(dy, dx, 1 - half) for dx, dy, half in order]


ARRIVALS = {
    (1, 0): X_UP,
    (-1, 0): X_DOWN,
    (0, 1): mirrored(X_UP),
    (0, -1): mirrored(X_DOWN),
}
LINKS = list(ARRIVALS)


def place_pieces():
    row, step_of = {}, {(0, 0, 0): 0, (0, 0, 1): 0}
    for step in range(1, STEPS + 1):
        free = {0: [0, 2], 1: [1, 3]}
        here = [order[step - 1] for order in ARRIVALS.values() if step <= len(order)]
        if step == STEPS:
            here = [(0, 0, 0), (0, 0, 1)] + here
        for piece in here:
            slot = free[piece[2]].pop(0)
            row[piece] = (step - 1) * CHUNK + slot * PIECE
            step_of.setdefault(piece, step)
    return row, step_of


ROW, STEP_OF = place_pieces()


def sends_by_step():
    out = [[] for _ in range(STEPS + 1)]
    for k, (lx, ly) in enumerate(LINKS):
        for i, (dx, dy, half) in enumerate(ARRIVALS[(lx, ly)]):
            mine = (wrap4(dx - lx), wrap4(dy - ly), half)
            out[STEP_OF[mine]].append((k, i, ROW[mine], ROW[(dx, dy, half)]))
    return out


PLANE_SENDS = sends_by_step()
PEERS = [(dx, dy) for dx in (0, 1, -1, 2) for dy in (0, 1, -1, 2) if (dx, dy) != (0, 0)]
Z_STEPS = 7
ROWS = 512
ITEMS = (
    [(0, 0), (1, 0), (2, 0), (0, 1), (1, 1), (2, 1), (3, 0), (3, 1), (4, 0), (4, 1)]
    + [(c, 2) for c in range(5)]
    + [(5, 0), (5, 1), (5, 2), (6, 0), (6, 1), (6, 2), (7, 0), (7, 1), (7, 2)]
    + [(7 - c, 3) for c in range(8)]
)
BEFORE = {
    0: ([1, 2], [0, 1]),
    2: ([3], [2, 3]),
    6: ([4], []),
    8: ([5], []),
    10: ([], [4, 5]),
    14: ([6], []),
    18: ([7], []),
    20: ([8], []),
    24: ([], [6, 7]),
}
OWN_ITEM = ITEMS.index((STEPS - 1, 0))


def item_at(n):
    chunk, block = jnp.int32(0), jnp.int32(0)
    for k, (c, b) in enumerate(ITEMS):
        chunk = jnp.where(n == k, c, chunk)
        block = jnp.where(n == k, b, block)
    return chunk, block


def peers_after(first_chunk, last_chunk):
    out = []
    for n, (dx, dy) in enumerate(PEERS):
        lowest = min(ROW[(dx, dy, half)] // CHUNK for half in (0, 1))
        if first_chunk <= lowest < last_chunk:
            out.append(n)
    return out


def tree_sum(values):
    while len(values) > 1:
        pairs = [a + b for a, b in zip(values[::2], values[1::2])]
        values = pairs + ([values[-1]] if len(values) % 2 else [])
    return values[0]


def kernel(
    log_total,
    samples,
    x_ref,
    order_ref,
    log_conn_ref,
    fit_ref,
    slope_ref,
    genes,
    partners,
    acc,
    tile_even,
    tile_odd,
    self_ref,
    outgoing,
    incoming,
    conn_ref,
    hist_ref,
    plane_ref,
    plane_hist,
    line_hist,
    core_hist,
    line_ref,
    results,
    fit_out,
    slope_out,
    local_sem,
    plane_send,
    plane_recv,
    z_send,
    z_recv,
    core_send,
    core_recv,
    part_send,
    part_recv,
    hist_send,
    hist_recv,
    line_send,
    line_recv,
    last_send,
    last_recv,
    out_sem,
):
    z, y, x, core = (lax.axis_index(a) for a in AXES)

    def at(dx=0, dy=0, dz=0, dc=0):
        return (
            lax.rem(z + (dz + 8), 8),
            lax.rem(y + (dy + 4), 4),
            lax.rem(x + (dx + 4), 4),
            lax.rem(core + dc, 2),
        )

    own_row = ROW[(0, 0, 0)]
    loads = []
    for k in range(SLABS):
        cols = pl.ds(k * LANES, LANES)
        loads.append(
            pltpu.make_async_copy(
                x_ref.at[:, cols], genes.at[k, pl.ds(own_row, 2 * PIECE), :], local_sem.at[0, k]
            )
        )
        loads.append(
            pltpu.make_async_copy(
                x_ref.at[:, cols], partners.at[k, pl.ds(0, 2 * PIECE), :], local_sem.at[1, k]
            )
        )
    for copy in loads:
        copy.start()

    barrier = pltpu.get_barrier_semaphore()
    near = [at(dx=1), at(dx=-1), at(dy=1), at(dy=-1), at(dz=1), at(dz=-1), at(dc=1)]
    for device in near:
        pl.semaphore_signal(barrier, inc=1, device_id=device, device_id_type=MESH_ID)
    acc[...] = jnp.zeros_like(acc)
    for copy in loads:
        copy.wait()
    pl.semaphore_wait(barrier, len(near))

    def remote(src, dst, send_sem, recv_sem, device):
        return pltpu.make_async_remote_copy(
            src_ref=src,
            dst_ref=dst,
            send_sem=send_sem,
            recv_sem=recv_sem,
            device_id=device,
            device_id_type=MESH_ID,
        )

    def plane_copy(k, i, src, dst):
        lx, ly = LINKS[k]
        return remote(
            genes.at[:, pl.ds(src, PIECE), :],
            genes.at[:, pl.ds(dst, PIECE), :],
            plane_send.at[k, i],
            plane_recv.at[k, i],
            at(dx=-lx, dy=-ly),
        )

    def z_row(direction, step):
        return step * CHUNK + (0 if direction == 1 else PIECE)

    def z_copy(direction, step):
        if step <= 2:
            first = step == 1
            src = 0 if first == (direction == 1) else PIECE
        else:
            src = z_row(direction, step - 2)
        side = 0 if direction == 1 else 1
        return remote(
            partners.at[:, pl.ds(src, PIECE), :],
            partners.at[:, pl.ds(z_row(direction, step), PIECE), :],
            z_send.at[side, step - 1],
            z_recv.at[side, step - 1],
            at(dz=-direction),
        )

    def core_copy(step):
        return remote(
            partners.at[:, pl.ds(step * CHUNK, 2 * PIECE), :],
            partners.at[:, pl.ds(step * CHUNK + 2 * PIECE, 2 * PIECE), :],
            core_send.at[step],
            core_recv.at[step],
            at(dc=1),
        )

    def communicate(step):
        if step:
            for k, link in enumerate(LINKS):
                if step <= len(ARRIVALS[link]):
                    plane_copy(k, step - 1, 0, ROW[ARRIVALS[link][step - 1]]).wait_recv()
            if step <= Z_STEPS:
                for direction in (1, -1):
                    z_copy(direction, step).wait_recv()
        for send in PLANE_SENDS[step]:
            plane_copy(*send).start()
        for later in (1, 2) if step == 0 else (step + 2,):
            if later <= Z_STEPS:
                for direction in (1, -1):
                    z_copy(direction, later).start()
        if step <= Z_STEPS:
            core_copy(step).start()

    def partner_rows_ready(step):
        core_copy(step).wait_recv()

    def lanes_of(ref, first, count):
        return jnp.concatenate(
            [ref[k, pl.ds(pl.multiple_of(first, PIECE), count), :] for k in range(SLABS)], axis=1
        )

    scale = 1.0 / samples

    def multiply(tile, item):
        chunk, block = item
        tile[pl.ds(0, ROWS), :] = lax.dot_general(
            lanes_of(partners, block * ROWS, ROWS),
            lanes_of(genes, chunk * CHUNK, CHUNK),
            (((1,), (1,)), ((), ())),
            preferred_element_type=jnp.float32,
        )

    def accumulate(tile, item):
        base = pl.multiple_of(item[0] * CHUNK, CHUNK)
        token = pl.multiple_of(ROWS + 8 * item[0], 8)
        for i in range(ROWS // 256):
            for j in range(CHUNK // LANES):
                magnitude = [
                    jnp.abs(
                        tile[pl.ds(i * 256 + q * 16, 16), pl.ds(j * LANES, LANES)].astype(
                            jnp.bfloat16
                        )
                        * scale
                    )
                    for q in range(16)
                ]
                current = magnitude
                for power in range(POWERS):
                    total = tree_sum(current).astype(jnp.float32)
                    total = total[0:8] + total[8:16]
                    acc[power, :, pl.ds(base + j * LANES, LANES)] += total
                    if power == TOKEN_POWER:
                        tile[pl.ds(token, 8), pl.ds(0, LANES)] = total
                    if power < POWERS - 1:
                        current = [a * b for a, b in zip(current, magnitude)]

    def keep_self_apart(tile):
        block = tile[pl.ds(0, 2 * PIECE), pl.ds(0, 2 * PIECE)]
        same = lax.broadcasted_iota(jnp.int32, block.shape, 0) == lax.broadcasted_iota(
            jnp.int32, block.shape, 1
        )
        own = jnp.sum(jnp.where(same, block, 0.0), axis=0, keepdims=True)
        self_ref[...] = jnp.abs(own) * scale
        tile[pl.ds(0, 2 * PIECE), pl.ds(0, 2 * PIECE)] = jnp.where(same, 0.0, block)

    low_half = lax.broadcasted_iota(jnp.int32, (POWERS, 8, LANES), 2) < PIECE

    def sums_of(dx, dy):
        low, high = (
            acc[:, :, pl.ds(ROW[(dx, dy, half)] // LANES * LANES, LANES)] for half in (0, 1)
        )
        return jnp.sum(jnp.where(low_half, low, high), axis=1)

    def part_copy(n):
        dx, dy = PEERS[n]
        return remote(
            outgoing.at[n], incoming.at[n], part_send.at[n], part_recv.at[n], at(dx=dx, dy=dy)
        )

    def send_parts(first_chunk, last_chunk):
        for n in peers_after(first_chunk, last_chunk):
            outgoing[n] = sums_of(*PEERS[n])
            part_copy(n).start()

    sends = {28: (5, 8), 30: (3, 5)}

    def prepare(u):
        for n in range(0, len(ITEMS), 2):
            if n in BEFORE or n in sends or n == OWN_ITEM + 1:

                @pl.when(u == n // 2)
                def _():
                    steps, rows = BEFORE.get(n, ([], []))
                    for step in steps:
                        communicate(step)
                    for step in rows:
                        partner_rows_ready(step)
                    if n == OWN_ITEM + 1:
                        keep_self_apart((tile_even, tile_odd)[OWN_ITEM % 2])
                    if n in sends:
                        send_parts(*sends[n])

    communicate(0)
    tile_odd[...] = jnp.zeros_like(tile_odd)

    def body(u, carry):
        prepare(u)
        multiply(tile_even, item_at(2 * u))
        accumulate(tile_odd, item_at(2 * u - 1))
        multiply(tile_odd, item_at(2 * u + 1))
        accumulate(tile_even, item_at(2 * u))
        return carry

    lax.fori_loop(0, len(ITEMS) // 2, body, 0)
    accumulate(tile_odd, item_at(jnp.int32(len(ITEMS) - 1)))
    send_parts(0, 3)
    total = sums_of(0, 0)
    own = self_ref[...]
    powers = [own]
    for _ in range(POWERS - 1):
        powers.append(powers[-1] * own)
    total = total + jnp.concatenate(powers, axis=0)
    for n in range(len(PEERS)):
        part_copy(n).wait_recv()
        total = total + incoming[n]
    conn_ref[...] = total
    picked = jnp.concatenate([conn_ref[pl.ds(order_ref[t], 1), :] for t in range(POWERS)], axis=0)
    log_conn = jnp.log(picked)
    results[pl.ds(0, POWERS), :] = log_conn
    out_copies = [pltpu.make_async_copy(results.at[pl.ds(0, POWERS), :], log_conn_ref, out_sem.at[0])]
    out_copies[0].start()

    position = log_conn * ((BINS - 1) / log_total)
    position = jnp.concatenate(
        [position, jnp.zeros((LANES - POWERS, LANES), jnp.float32)], axis=0
    ).T
    levels = lax.broadcasted_iota(jnp.int32, (LANES, BINS), 1).astype(jnp.float32)
    for t in range(POWERS):
        weights = jnp.maximum(0.0, 1.0 - jnp.abs(position[:, t : t + 1] - levels))
        hist_ref[pl.ds(t, 1), :] = jnp.sum(weights, axis=0, keepdims=True)

    here = x * 4 + y

    def hist_copy(n, src):
        dx, dy = PEERS[n]
        return remote(
            hist_ref, plane_hist.at[src], hist_send.at[n], hist_recv.at[n], at(dx=dx, dy=dy)
        )

    for n in range(len(PEERS)):
        hist_copy(n, here).start()
    plane_hist[here] = hist_ref[...]
    for n in range(len(PEERS)):
        dx, dy = PEERS[n]
        hist_copy(n, lax.rem(x + (4 - dx), 4) * 4 + lax.rem(y + (4 - dy), 4)).wait_recv()
    plane_ref[...] = tree_sum([plane_hist[i] for i in range(16)])

    def line_copy(n, src):
        return remote(
            plane_ref, line_hist.at[src], line_send.at[n], line_recv.at[n], at(dz=n + 1)
        )

    for n in range(7):
        line_copy(n, z).start()
    line_hist[z] = plane_ref[...]
    for n in range(7):
        line_copy(n, lax.rem(z + (7 - n), 8)).wait_recv()
    line_ref[...] = tree_sum([line_hist[i] for i in range(8)])
    last = remote(line_ref, core_hist, last_send, last_recv, at(dc=1))
    last.start()
    last.wait_recv()
    hist = line_ref[...] + core_hist[...]

    hist = jnp.concatenate([hist, jnp.zeros((LANES - POWERS, BINS), jnp.float32)], axis=0).T
    centers = lax.broadcasted_iota(jnp.int32, hist.shape, 0).astype(jnp.float32) * (
        log_total / (BINS - 1)
    )

    def over_bins(value):
        return jnp.sum(value, axis=0, keepdims=True)

    weight_sum = over_bins(hist)
    ylog = jnp.log(hist + 1.0) - log_total
    xdev = centers - over_bins(hist * centers) / weight_sum
    ydev = ylog - over_bins(hist * ylog) / weight_sum
    sxx = jnp.maximum(over_bins(hist * xdev * xdev) / weight_sum, 0.05)
    syy = jnp.maximum(over_bins(hist * ydev * ydev) / weight_sum, 0.05)
    sxy = over_bins(hist * xdev * ydev) / weight_sum
    fit_out[...] = (-sxy * jnp.abs(sxy) / (sxx * syy))[:, :POWERS]
    slope_out[...] = (sxy / sxx)[:, :POWERS]
    out_copies.append(pltpu.make_async_copy(fit_out, fit_ref, out_sem.at[1]))
    out_copies.append(pltpu.make_async_copy(slope_out, slope_ref, out_sem.at[2]))
    for copy in out_copies[1:]:
        copy.start()
    for sends in PLANE_SENDS:
        for send in sends:
            plane_copy(*send).wait_send()
    for step in range(1, Z_STEPS + 1):
        for direction in (1, -1):
            z_copy(direction, step).wait_send()
    for step in range(Z_STEPS + 1):
        core_copy(step).wait_send()
    for n in range(len(PEERS)):
        part_copy(n).wait_send()
        hist_copy(n, here).wait_send()
    for n in range(7):
        line_copy(n, z).wait_send()
    last.wait_send()
    for copy in out_copies:
        copy.wait()


def on_device(expression, power_order):
    genes_dev, samples = expression.shape
    powers = power_order.shape[0]
    total_genes = genes_dev * lax.axis_size(AXES)
    plane, line = len(PEERS), 7
    dma = pltpu.SemaphoreType.DMA
    log_conn, fit, slope = pl.pallas_call(
        functools.partial(kernel, math.log(total_genes), samples),
        out_shape=(
            jax.ShapeDtypeStruct((powers, genes_dev), jnp.float32),
            jax.ShapeDtypeStruct((1, powers), jnp.float32),
            jax.ShapeDtypeStruct((1, powers), jnp.float32),
        ),
        in_specs=[pl.BlockSpec(memory_space=pltpu.HBM), pl.BlockSpec(memory_space=pltpu.SMEM)],
        out_specs=(pl.BlockSpec(memory_space=pltpu.HBM),) * 3,
        scratch_shapes=[
            pltpu.VMEM((SLABS, 2048, LANES), jnp.bfloat16),
            pltpu.VMEM((SLABS, 2048, LANES), jnp.bfloat16),
            pltpu.VMEM((POWERS, 8, 2048), jnp.float32),
            pltpu.VMEM((ROWS + 8 * STEPS, CHUNK), jnp.float32),
            pltpu.VMEM((ROWS + 8 * STEPS, CHUNK), jnp.float32),
            pltpu.VMEM((1, LANES), jnp.float32),
            pltpu.VMEM((plane, powers, LANES), jnp.float32),
            pltpu.VMEM((plane, powers, LANES), jnp.float32),
            pltpu.VMEM((powers, LANES), jnp.float32),
            pltpu.VMEM((powers, BINS), jnp.float32),
            pltpu.VMEM((powers, BINS), jnp.float32),
            pltpu.VMEM((16, powers, BINS), jnp.float32),
            pltpu.VMEM((8, powers, BINS), jnp.float32),
            pltpu.VMEM((powers, BINS), jnp.float32),
            pltpu.VMEM((powers, BINS), jnp.float32),
            pltpu.VMEM((powers, LANES), jnp.float32),
            pltpu.VMEM((1, powers), jnp.float32),
            pltpu.VMEM((1, powers), jnp.float32),
            dma((2, SLABS)),
            dma((4, STEPS)),
            dma((4, STEPS)),
            dma((2, Z_STEPS)),
            dma((2, Z_STEPS)),
            dma((STEPS,)),
            dma((STEPS,)),
            dma((plane,)),
            dma((plane,)),
            dma((plane,)),
            dma((plane,)),
            dma((line,)),
            dma((line,)),
            dma,
            dma,
            dma((3,)),
        ],
        compiler_params=pltpu.CompilerParams(
            collective_id=0, has_side_effects=True, vmem_limit_bytes=67_043_328
        ),
        name="coexpression",
    )(expression, power_order)
    return log_conn.T, fit.reshape(powers), slope.reshape(powers)


def solution(mesh):
    torus = Mesh(mesh.devices.reshape(8, 4, 4, 2), AXES)
    along = P(AXES, None)
    return jax.shard_map(
        on_device,
        mesh=torus,
        in_specs=(along, P()),
        out_specs=(along, P(), P()),
        check_vma=False,
    )
```

```python
import functools
import math

import jax
import jax.numpy as jnp
from jax import lax
from jax.experimental import pallas as pl
from jax.experimental.pallas import tpu as pltpu
from jax.sharding import Mesh
from jax.sharding import PartitionSpec as P

AXES = ("row_0", "row_1", "col_0", "col_1")
POWERS = 20
BINS = 128
LANES = 128
SLABS = 8
PIECE = 64
CHUNK = 256
STEPS = 8
SHARES = 4
MESH_ID = pl.DeviceIdType.MESH


def wrap4(d):
    return {0: 0, 1: 1, 2: 2, 3: -1}[d % 4]


X_UP = [(1, 0, 0), (1, 0, 1), (2, 0, 0), (1, 1, 1), (1, -1, 1), (2, 0, 1), (1, 2, 1)]
X_DOWN = [(-1, 0, 0), (-1, 0, 1), (-1, 1, 1), (-1, -1, 1), (-1, 2, 1), (2, 1, 1), (2, -1, 1), (2, 2, 1)]


def mirrored(order):
    return [(dy, dx, 1 - half) for dx, dy, half in order]


ARRIVALS = {
    (1, 0): X_UP,
    (-1, 0): X_DOWN,
    (0, 1): mirrored(X_UP),
    (0, -1): mirrored(X_DOWN),
}
LINKS = list(ARRIVALS)


def place_pieces():
    row, step_of = {}, {(0, 0, 0): 0, (0, 0, 1): 0}
    for step in range(1, STEPS + 1):
        free = {0: [0, 2], 1: [1, 3]}
        here = [order[step - 1] for order in ARRIVALS.values() if step <= len(order)]
        if step == STEPS:
            here = [(0, 0, 0), (0, 0, 1)] + here
        for piece in here:
            slot = free[piece[2]].pop(0)
            row[piece] = (step - 1) * CHUNK + slot * PIECE
            step_of.setdefault(piece, step)
    return row, step_of


ROW, STEP_OF = place_pieces()


def sends_by_step():
    out = [[] for _ in range(STEPS + 1)]
    for k, (lx, ly) in enumerate(LINKS):
        for i, (dx, dy, half) in enumerate(ARRIVALS[(lx, ly)]):
            mine = (wrap4(dx - lx), wrap4(dy - ly), half)
            out[STEP_OF[mine]].append((k, i, ROW[mine], ROW[(dx, dy, half)]))
    return out


PLANE_SENDS = sends_by_step()
PEERS = [(dx, dy) for dx in (0, 1, -1, 2) for dy in (0, 1, -1, 2) if (dx, dy) != (0, 0)]
Z_STEPS = 7
ROWS = 512
ITEMS = (
    [(0, 0), (1, 0), (2, 0), (0, 1), (1, 1), (2, 1), (3, 0), (3, 1), (4, 0), (4, 1)]
    + [(c, 2) for c in range(5)]
    + [(5, 0), (5, 1), (5, 2), (6, 0), (6, 1), (6, 2), (6, 3), (5, 3), (4, 3)]
    + [(7, 1), (7, 0), (7, 2), (7, 3), (3, 3), (2, 3), (1, 3), (0, 3)]
)
BEFORE = {
    0: ([1, 2], [0, 1]),
    2: ([3], [2, 3]),
    6: ([4], []),
    8: ([5], []),
    10: ([], [4, 5]),
    14: ([6], []),
    18: ([7], []),
    20: ([], [6, 7]),
    24: ([8], []),
}
OWN_ITEM = ITEMS.index((STEPS - 1, 0))


def item_at(n):
    chunk, block = jnp.int32(0), jnp.int32(0)
    for k, (c, b) in enumerate(ITEMS):
        chunk = jnp.where(n == k, c, chunk)
        block = jnp.where(n == k, b, block)
    return chunk, block


def sends_before():
    bounds = [28, 30, len(ITEMS) + 2]
    out = {n: [] for n in bounds}
    for peer, (dx, dy) in enumerate(PEERS):
        chunks = [ROW[(dx, dy, half)] // CHUNK for half in (0, 1)]
        done = max(n for n, (chunk, _) in enumerate(ITEMS) if chunk in chunks)
        out[min(n for n in bounds if n - 2 >= done)].append(peer)
    return out


PART_SENDS = sends_before()


def tree_sum(values):
    while len(values) > 1:
        pairs = [a + b for a, b in zip(values[::2], values[1::2])]
        values = pairs + ([values[-1]] if len(values) % 2 else [])
    return values[0]


def kernel(
    log_total,
    samples,
    x_ref,
    order_ref,
    log_conn_ref,
    fit_ref,
    slope_ref,
    genes,
    partners,
    acc,
    tile_even,
    tile_odd,
    self_ref,
    outgoing,
    incoming,
    conn_ref,
    hist_ref,
    plane_ref,
    plane_hist,
    line_hist,
    core_hist,
    line_ref,
    results,
    fit_out,
    slope_out,
    local_sem,
    plane_send,
    plane_recv,
    z_send,
    z_recv,
    core_send,
    core_recv,
    part_send,
    part_recv,
    hist_send,
    hist_recv,
    line_send,
    line_recv,
    last_send,
    last_recv,
    out_sem,
):
    z, y, x, core = (lax.axis_index(a) for a in AXES)

    def at(dx=0, dy=0, dz=0, dc=0):
        return (
            lax.rem(z + (dz + 8), 8),
            lax.rem(y + (dy + 4), 4),
            lax.rem(x + (dx + 4), 4),
            lax.rem(core + dc, 2),
        )

    own_row = ROW[(0, 0, 0)]
    loads = []
    for k in range(SLABS):
        cols = pl.ds(k * LANES, LANES)
        loads.append(
            pltpu.make_async_copy(
                x_ref.at[:, cols], genes.at[k, pl.ds(own_row, 2 * PIECE), :], local_sem.at[0, k]
            )
        )
        loads.append(
            pltpu.make_async_copy(
                x_ref.at[:, cols], partners.at[k, pl.ds(0, 2 * PIECE), :], local_sem.at[1, k]
            )
        )
    for copy in loads:
        copy.start()

    barrier = pltpu.get_barrier_semaphore()
    near = [at(dx=1), at(dx=-1), at(dy=1), at(dy=-1), at(dz=1), at(dz=-1), at(dc=1)]
    for device in near:
        pl.semaphore_signal(barrier, inc=1, device_id=device, device_id_type=MESH_ID)
    acc[...] = jnp.zeros_like(acc)
    for copy in loads:
        copy.wait()
    pl.semaphore_wait(barrier, len(near))

    def remote(src, dst, send_sem, recv_sem, device):
        return pltpu.make_async_remote_copy(
            src_ref=src,
            dst_ref=dst,
            send_sem=send_sem,
            recv_sem=recv_sem,
            device_id=device,
            device_id_type=MESH_ID,
        )

    def plane_copy(k, i, src, dst):
        lx, ly = LINKS[k]
        return remote(
            genes.at[:, pl.ds(src, PIECE), :],
            genes.at[:, pl.ds(dst, PIECE), :],
            plane_send.at[k, i],
            plane_recv.at[k, i],
            at(dx=-lx, dy=-ly),
        )

    def z_row(direction, step):
        return step * CHUNK + (0 if direction == 1 else PIECE)

    def z_copy(direction, step):
        if step <= 2:
            first = step == 1
            src = 0 if first == (direction == 1) else PIECE
        else:
            src = z_row(direction, step - 2)
        side = 0 if direction == 1 else 1
        return remote(
            partners.at[:, pl.ds(src, PIECE), :],
            partners.at[:, pl.ds(z_row(direction, step), PIECE), :],
            z_send.at[side, step - 1],
            z_recv.at[side, step - 1],
            at(dz=-direction),
        )

    def core_copy(step):
        return remote(
            partners.at[:, pl.ds(step * CHUNK, 2 * PIECE), :],
            partners.at[:, pl.ds(step * CHUNK + 2 * PIECE, 2 * PIECE), :],
            core_send.at[step],
            core_recv.at[step],
            at(dc=1),
        )

    def communicate(step):
        if step:
            for k, link in enumerate(LINKS):
                if step <= len(ARRIVALS[link]):
                    plane_copy(k, step - 1, 0, ROW[ARRIVALS[link][step - 1]]).wait_recv()
            if step <= Z_STEPS:
                for direction in (1, -1):
                    z_copy(direction, step).wait_recv()
        for send in PLANE_SENDS[step]:
            plane_copy(*send).start()
        for later in (1, 2) if step == 0 else (step + 2,):
            if later <= Z_STEPS:
                for direction in (1, -1):
                    z_copy(direction, later).start()
        if step <= Z_STEPS:
            core_copy(step).start()

    def partner_rows_ready(step):
        core_copy(step).wait_recv()

    def lanes_of(ref, first, count, part):
        slabs = range(part * SLABS // SHARES, (part + 1) * SLABS // SHARES)
        return jnp.concatenate(
            [ref[k, pl.ds(pl.multiple_of(first, PIECE), count), :] for k in slabs], axis=1
        )

    scale = 1.0 / samples

    def multiply(tile, item, part):
        chunk, block = item
        product = lax.dot_general(
            lanes_of(partners, block * ROWS, ROWS, part),
            lanes_of(genes, chunk * CHUNK, CHUNK, part),
            (((1,), (1,)), ((), ())),
            preferred_element_type=jnp.float32,
        )
        if part == 0:
            tile[pl.ds(0, ROWS), :] = product
        else:
            tile[pl.ds(0, ROWS), :] += product
        return product[ROWS - 8 :, :LANES]

    def accumulate(tile, item, unit):
        base = pl.multiple_of(item[0] * CHUNK, CHUNK)
        i, j = divmod(unit, CHUNK // LANES)
        magnitude = [
            jnp.abs(
                tile[pl.ds(i * 256 + q * 16, 16), pl.ds(j * LANES, LANES)].astype(jnp.bfloat16)
                * scale
            )
            for q in range(16)
        ]
        current = magnitude
        for power in range(POWERS):
            total = tree_sum(current).astype(jnp.float32)
            acc[power, :, pl.ds(base + j * LANES, LANES)] += total[0:8] + total[8:16]
            if power < POWERS - 1:
                current = [a * b for a, b in zip(current, magnitude)]

    def advance(tile, item, done_tile, done_item):
        row = pl.multiple_of(ROWS + 8 * done_item[0], 8)
        for share in range(SHARES):
            last = multiply(tile, item, share)
            accumulate(done_tile, done_item, share)
            if share < SHARES - 1:
                done_tile[pl.ds(row, 8), pl.ds(0, LANES)] = last

    def keep_self_apart(tile):
        block = tile[pl.ds(0, 2 * PIECE), pl.ds(0, 2 * PIECE)]
        same = lax.broadcasted_iota(jnp.int32, block.shape, 0) == lax.broadcasted_iota(
            jnp.int32, block.shape, 1
        )
        own = jnp.sum(jnp.where(same, block, 0.0), axis=0, keepdims=True)
        self_ref[...] = jnp.abs(own) * scale
        tile[pl.ds(0, 2 * PIECE), pl.ds(0, 2 * PIECE)] = jnp.where(same, 0.0, block)

    low_half = lax.broadcasted_iota(jnp.int32, (POWERS, 8, LANES), 2) < PIECE

    def sums_of(dx, dy):
        low, high = (
            acc[:, :, pl.ds(ROW[(dx, dy, half)] // LANES * LANES, LANES)] for half in (0, 1)
        )
        return jnp.sum(jnp.where(low_half, low, high), axis=1)

    def part_copy(n):
        dx, dy = PEERS[n]
        return remote(
            outgoing.at[n], incoming.at[n], part_send.at[n], part_recv.at[n], at(dx=dx, dy=dy)
        )

    def send_parts(before):
        for n in PART_SENDS[before]:
            outgoing[n] = sums_of(*PEERS[n])
            part_copy(n).start()

    def prepare(u):
        for n in range(0, len(ITEMS), 2):
            if n in BEFORE or n in PART_SENDS or n == OWN_ITEM + 1:

                @pl.when(u == n // 2)
                def _():
                    steps, rows = BEFORE.get(n, ([], []))
                    for step in steps:
                        communicate(step)
                    for step in rows:
                        partner_rows_ready(step)
                    if n == OWN_ITEM + 1:
                        keep_self_apart((tile_even, tile_odd)[OWN_ITEM % 2])
                    if n in PART_SENDS:
                        send_parts(n)

    communicate(0)
    tile_odd[...] = jnp.zeros_like(tile_odd)

    def body(u, carry):
        before, first, second = carry
        prepare(u)
        advance(tile_even, first, tile_odd, before)
        advance(tile_odd, second, tile_even, first)
        return second, item_at(2 * u + 2), item_at(2 * u + 3)

    lax.fori_loop(
        0, len(ITEMS) // 2, body, tuple(item_at(jnp.int32(n)) for n in (-1, 0, 1))
    )
    for unit in range(SHARES):
        accumulate(tile_odd, item_at(jnp.int32(len(ITEMS) - 1)), unit)
    send_parts(len(ITEMS) + 2)
    total = sums_of(0, 0)
    own = self_ref[...]
    powers = [own]
    for _ in range(POWERS - 1):
        powers.append(powers[-1] * own)
    total = total + jnp.concatenate(powers, axis=0)
    for n in range(len(PEERS)):
        part_copy(n).wait_recv()
        total = total + incoming[n]
    conn_ref[...] = total
    picked = jnp.concatenate([conn_ref[pl.ds(order_ref[t], 1), :] for t in range(POWERS)], axis=0)
    log_conn = jnp.log(picked)
    results[pl.ds(0, POWERS), :] = log_conn
    out_copies = [pltpu.make_async_copy(results.at[pl.ds(0, POWERS), :], log_conn_ref, out_sem.at[0])]
    out_copies[0].start()

    position = log_conn * ((BINS - 1) / log_total)
    position = jnp.concatenate(
        [position, jnp.zeros((LANES - POWERS, LANES), jnp.float32)], axis=0
    ).T
    levels = lax.broadcasted_iota(jnp.int32, (LANES, BINS), 1).astype(jnp.float32)
    for t in range(POWERS):
        weights = jnp.maximum(0.0, 1.0 - jnp.abs(position[:, t : t + 1] - levels))
        hist_ref[pl.ds(t, 1), :] = jnp.sum(weights, axis=0, keepdims=True)

    here = x * 4 + y

    def hist_copy(n, src):
        dx, dy = PEERS[n]
        return remote(
            hist_ref, plane_hist.at[src], hist_send.at[n], hist_recv.at[n], at(dx=dx, dy=dy)
        )

    for n in range(len(PEERS)):
        hist_copy(n, here).start()
    plane_hist[here] = hist_ref[...]
    for n in range(len(PEERS)):
        dx, dy = PEERS[n]
        hist_copy(n, lax.rem(x + (4 - dx), 4) * 4 + lax.rem(y + (4 - dy), 4)).wait_recv()
    plane_ref[...] = tree_sum([plane_hist[i] for i in range(16)])

    def line_copy(n, src):
        return remote(
            plane_ref, line_hist.at[src], line_send.at[n], line_recv.at[n], at(dz=n + 1)
        )

    for n in range(7):
        line_copy(n, z).start()
    line_hist[z] = plane_ref[...]
    for n in range(7):
        line_copy(n, lax.rem(z + (7 - n), 8)).wait_recv()
    line_ref[...] = tree_sum([line_hist[i] for i in range(8)])
    last = remote(line_ref, core_hist, last_send, last_recv, at(dc=1))
    last.start()
    last.wait_recv()
    hist = line_ref[...] + core_hist[...]

    hist = jnp.concatenate([hist, jnp.zeros((LANES - POWERS, BINS), jnp.float32)], axis=0).T
    centers = lax.broadcasted_iota(jnp.int32, hist.shape, 0).astype(jnp.float32) * (
        log_total / (BINS - 1)
    )

    def over_bins(value):
        return jnp.sum(value, axis=0, keepdims=True)

    weight_sum = over_bins(hist)
    ylog = jnp.log(hist + 1.0) - log_total
    xdev = centers - over_bins(hist * centers) / weight_sum
    ydev = ylog - over_bins(hist * ylog) / weight_sum
    sxx = jnp.maximum(over_bins(hist * xdev * xdev) / weight_sum, 0.05)
    syy = jnp.maximum(over_bins(hist * ydev * ydev) / weight_sum, 0.05)
    sxy = over_bins(hist * xdev * ydev) / weight_sum
    fit_out[...] = (-sxy * jnp.abs(sxy) / (sxx * syy))[:, :POWERS]
    slope_out[...] = (sxy / sxx)[:, :POWERS]
    out_copies.append(pltpu.make_async_copy(fit_out, fit_ref, out_sem.at[1]))
    out_copies.append(pltpu.make_async_copy(slope_out, slope_ref, out_sem.at[2]))
    for copy in out_copies[1:]:
        copy.start()
    for sends in PLANE_SENDS:
        for send in sends:
            plane_copy(*send).wait_send()
    for step in range(1, Z_STEPS + 1):
        for direction in (1, -1):
            z_copy(direction, step).wait_send()
    for step in range(Z_STEPS + 1):
        core_copy(step).wait_send()
    for n in range(len(PEERS)):
        part_copy(n).wait_send()
        hist_copy(n, here).wait_send()
    for n in range(7):
        line_copy(n, z).wait_send()
    last.wait_send()
    for copy in out_copies:
        copy.wait()


def on_device(expression, power_order):
    genes_dev, samples = expression.shape
    powers = power_order.shape[0]
    total_genes = genes_dev * lax.axis_size(AXES)
    plane, line = len(PEERS), 7
    dma = pltpu.SemaphoreType.DMA
    log_conn, fit, slope = pl.pallas_call(
        functools.partial(kernel, math.log(total_genes), samples),
        out_shape=(
            jax.ShapeDtypeStruct((powers, genes_dev), jnp.float32),
            jax.ShapeDtypeStruct((1, powers), jnp.float32),
            jax.ShapeDtypeStruct((1, powers), jnp.float32),
        ),
        in_specs=[pl.BlockSpec(memory_space=pltpu.HBM), pl.BlockSpec(memory_space=pltpu.SMEM)],
        out_specs=(pl.BlockSpec(memory_space=pltpu.HBM),) * 3,
        scratch_shapes=[
            pltpu.VMEM((SLABS, 2048, LANES), jnp.bfloat16),
            pltpu.VMEM((SLABS, 2048, LANES), jnp.bfloat16),
            pltpu.VMEM((POWERS, 8, 2048), jnp.float32),
            pltpu.VMEM((ROWS + 8 * STEPS, CHUNK), jnp.float32),
            pltpu.VMEM((ROWS + 8 * STEPS, CHUNK), jnp.float32),
            pltpu.VMEM((1, LANES), jnp.float32),
            pltpu.VMEM((plane, powers, LANES), jnp.float32),
            pltpu.VMEM((plane, powers, LANES), jnp.float32),
            pltpu.VMEM((powers, LANES), jnp.float32),
            pltpu.VMEM((powers, BINS), jnp.float32),
            pltpu.VMEM((powers, BINS), jnp.float32),
            pltpu.VMEM((16, powers, BINS), jnp.float32),
            pltpu.VMEM((8, powers, BINS), jnp.float32),
            pltpu.VMEM((powers, BINS), jnp.float32),
            pltpu.VMEM((powers, BINS), jnp.float32),
            pltpu.VMEM((powers, LANES), jnp.float32),
            pltpu.VMEM((1, powers), jnp.float32),
            pltpu.VMEM((1, powers), jnp.float32),
            dma((2, SLABS)),
            dma((4, STEPS)),
            dma((4, STEPS)),
            dma((2, Z_STEPS)),
            dma((2, Z_STEPS)),
            dma((STEPS,)),
            dma((STEPS,)),
            dma((plane,)),
            dma((plane,)),
            dma((plane,)),
            dma((plane,)),
            dma((line,)),
            dma((line,)),
            dma,
            dma,
            dma((3,)),
        ],
        compiler_params=pltpu.CompilerParams(
            collective_id=0, has_side_effects=True, vmem_limit_bytes=66_800_000
        ),
        name="coexpression",
    )(expression, power_order)
    return log_conn.T, fit.reshape(powers), slope.reshape(powers)


def solution(mesh):
    torus = Mesh(mesh.devices.reshape(8, 4, 4, 2), AXES)
    along = P(AXES, None)
    return jax.shard_map(
        on_device,
        mesh=torus,
        in_specs=(along, P()),
        out_specs=(along, P(), P()),
        check_vma=False,
    )
```

```python
import functools
import math

import jax
import jax.numpy as jnp
from jax import lax
from jax.experimental import pallas as pl
from jax.experimental.pallas import tpu as pltpu
from jax.sharding import Mesh
from jax.sharding import PartitionSpec as P

AXES = ("row_0", "row_1", "col_0", "col_1")
POWERS = 20
BINS = 128
LANES = 128
SLABS = 8
PIECE = 64
CHUNK = 256
STEPS = 8
SHARES = 4
MESH_ID = pl.DeviceIdType.MESH


def wrap4(d):
    return {0: 0, 1: 1, 2: 2, 3: -1}[d % 4]


X_UP = [(1, 0, 0), (1, 0, 1), (2, 0, 0), (1, 1, 1), (1, -1, 1), (2, 0, 1), (1, 2, 1)]
X_DOWN = [(-1, 0, 0), (-1, 0, 1), (-1, 1, 1), (-1, -1, 1), (-1, 2, 1), (2, 1, 1), (2, -1, 1), (2, 2, 1)]


def mirrored(order):
    return [(dy, dx, 1 - half) for dx, dy, half in order]


ARRIVALS = {
    (1, 0): X_UP,
    (-1, 0): X_DOWN,
    (0, 1): mirrored(X_UP),
    (0, -1): mirrored(X_DOWN),
}
LINKS = list(ARRIVALS)


def place_pieces():
    row, step_of = {}, {(0, 0, 0): 0, (0, 0, 1): 0}
    for step in range(1, STEPS + 1):
        free = {0: [0, 2], 1: [1, 3]}
        here = [order[step - 1] for order in ARRIVALS.values() if step <= len(order)]
        if step == STEPS:
            here = [(0, 0, 0), (0, 0, 1)] + here
        for piece in here:
            slot = free[piece[2]].pop(0)
            row[piece] = (step - 1) * CHUNK + slot * PIECE
            step_of.setdefault(piece, step)
    return row, step_of


ROW, STEP_OF = place_pieces()


def sends_by_step():
    out = [[] for _ in range(STEPS + 1)]
    for k, (lx, ly) in enumerate(LINKS):
        for i, (dx, dy, half) in enumerate(ARRIVALS[(lx, ly)]):
            mine = (wrap4(dx - lx), wrap4(dy - ly), half)
            out[STEP_OF[mine]].append((k, i, ROW[mine], ROW[(dx, dy, half)]))
    return out


PLANE_SENDS = sends_by_step()
PEERS = sorted(
    [(dx, dy) for dx in (0, 1, -1, 2) for dy in (0, 1, -1, 2) if (dx, dy) != (0, 0)],
    key=lambda peer: -abs(peer[0]) - abs(peer[1]),
)
LINE_PEERS = (4, 3, 5, 2, 6, 1, 7)
Z_STEPS = 7
ROWS = 512
ITEMS = (
    [(0, 0), (1, 0), (2, 0), (0, 1), (1, 1), (2, 1), (3, 0), (3, 1), (4, 0), (4, 1)]
    + [(c, 2) for c in range(5)]
    + [(5, 0), (5, 1), (5, 2), (6, 0), (6, 1), (6, 2), (6, 3), (5, 3), (4, 3)]
    + [(7, 1), (7, 0), (7, 2), (7, 3), (3, 3), (2, 3), (1, 3), (0, 3)]
)
BEFORE = {
    0: ([1, 2], [0, 1]),
    2: ([3], [2, 3]),
    6: ([4], []),
    8: ([5], []),
    10: ([], [4, 5]),
    14: ([6], []),
    18: ([7], []),
    20: ([], [6, 7]),
    24: ([8], []),
}
OWN_ITEM = ITEMS.index((STEPS - 1, 0))


def item_at(n):
    chunk, block = jnp.int32(0), jnp.int32(0)
    for k, (c, b) in enumerate(ITEMS):
        chunk = jnp.where(n == k, c, chunk)
        block = jnp.where(n == k, b, block)
    return chunk, block


def sends_before():
    bounds = [28, 30, len(ITEMS) + 2]
    out = {n: [] for n in bounds}
    for peer, (dx, dy) in enumerate(PEERS):
        chunks = [ROW[(dx, dy, half)] // CHUNK for half in (0, 1)]
        done = max(n for n, (chunk, _) in enumerate(ITEMS) if chunk in chunks)
        out[min(n for n in bounds if n - 2 >= done)].append(peer)
    return out


PART_SENDS = sends_before()


def tree_sum(values):
    while len(values) > 1:
        pairs = [a + b for a, b in zip(values[::2], values[1::2])]
        values = pairs + ([values[-1]] if len(values) % 2 else [])
    return values[0]


def kernel(
    log_total,
    samples,
    x_ref,
    order_ref,
    log_conn_ref,
    fit_ref,
    slope_ref,
    genes,
    partners,
    acc,
    tile_even,
    tile_odd,
    self_ref,
    outgoing,
    incoming,
    conn_ref,
    hist_ref,
    plane_ref,
    plane_hist,
    line_hist,
    core_hist,
    line_ref,
    results,
    fit_out,
    slope_out,
    local_sem,
    plane_send,
    plane_recv,
    z_send,
    z_recv,
    core_send,
    core_recv,
    part_send,
    part_recv,
    hist_send,
    hist_recv,
    line_send,
    line_recv,
    last_send,
    last_recv,
    out_sem,
):
    z, y, x, core = (lax.axis_index(a) for a in AXES)

    def at(dx=0, dy=0, dz=0, dc=0):
        return (
            lax.rem(z + (dz + 8), 8),
            lax.rem(y + (dy + 4), 4),
            lax.rem(x + (dx + 4), 4),
            lax.rem(core + dc, 2),
        )

    own_row = ROW[(0, 0, 0)]
    loads = []
    for k in range(SLABS):
        cols = pl.ds(k * LANES, LANES)
        loads.append(
            pltpu.make_async_copy(
                x_ref.at[:, cols], genes.at[k, pl.ds(own_row, 2 * PIECE), :], local_sem.at[0, k]
            )
        )
        loads.append(
            pltpu.make_async_copy(
                x_ref.at[:, cols], partners.at[k, pl.ds(0, 2 * PIECE), :], local_sem.at[1, k]
            )
        )
    for copy in loads:
        copy.start()

    barrier = pltpu.get_barrier_semaphore()
    near = [at(dx=1), at(dx=-1), at(dy=1), at(dy=-1), at(dz=1), at(dz=-1), at(dc=1)]
    for device in near:
        pl.semaphore_signal(barrier, inc=1, device_id=device, device_id_type=MESH_ID)
    acc[...] = jnp.zeros_like(acc)
    for copy in loads:
        copy.wait()
    pl.semaphore_wait(barrier, len(near))

    def remote(src, dst, send_sem, recv_sem, device):
        return pltpu.make_async_remote_copy(
            src_ref=src,
            dst_ref=dst,
            send_sem=send_sem,
            recv_sem=recv_sem,
            device_id=device,
            device_id_type=MESH_ID,
        )

    def plane_copy(k, i, src, dst):
        lx, ly = LINKS[k]
        return remote(
            genes.at[:, pl.ds(src, PIECE), :],
            genes.at[:, pl.ds(dst, PIECE), :],
            plane_send.at[k, i],
            plane_recv.at[k, i],
            at(dx=-lx, dy=-ly),
        )

    def z_row(direction, step):
        return step * CHUNK + (0 if direction == 1 else PIECE)

    def z_copy(direction, step):
        if step <= 2:
            first = step == 1
            src = 0 if first == (direction == 1) else PIECE
        else:
            src = z_row(direction, step - 2)
        side = 0 if direction == 1 else 1
        return remote(
            partners.at[:, pl.ds(src, PIECE), :],
            partners.at[:, pl.ds(z_row(direction, step), PIECE), :],
            z_send.at[side, step - 1],
            z_recv.at[side, step - 1],
            at(dz=-direction),
        )

    def core_copy(step):
        return remote(
            partners.at[:, pl.ds(step * CHUNK, 2 * PIECE), :],
            partners.at[:, pl.ds(step * CHUNK + 2 * PIECE, 2 * PIECE), :],
            core_send.at[step],
            core_recv.at[step],
            at(dc=1),
        )

    def communicate(step):
        if step:
            for k, link in enumerate(LINKS):
                if step <= len(ARRIVALS[link]):
                    plane_copy(k, step - 1, 0, ROW[ARRIVALS[link][step - 1]]).wait_recv()
            if step <= Z_STEPS:
                for direction in (1, -1):
                    z_copy(direction, step).wait_recv()
        for send in PLANE_SENDS[step]:
            plane_copy(*send).start()
        for later in (1, 2) if step == 0 else (step + 2,):
            if later <= Z_STEPS:
                for direction in (1, -1):
                    z_copy(direction, later).start()
        if step <= Z_STEPS:
            core_copy(step).start()

    def partner_rows_ready(step):
        core_copy(step).wait_recv()

    def lanes_of(ref, first, count, part):
        slabs = range(part * SLABS // SHARES, (part + 1) * SLABS // SHARES)
        return jnp.concatenate(
            [ref[k, pl.ds(pl.multiple_of(first, PIECE), count), :] for k in slabs], axis=1
        )

    scale = 1.0 / samples

    def multiply(tile, item, part):
        chunk, block = item
        product = lax.dot_general(
            lanes_of(partners, block * ROWS, ROWS, part),
            lanes_of(genes, chunk * CHUNK, CHUNK, part),
            (((1,), (1,)), ((), ())),
            preferred_element_type=jnp.float32,
        )
        if part == 0:
            tile[pl.ds(0, ROWS), :] = product
        else:
            tile[pl.ds(0, ROWS), :] += product
        return product[ROWS - 8 :, :LANES]

    def accumulate(tile, item, unit):
        base = pl.multiple_of(item[0] * CHUNK, CHUNK)
        i, j = divmod(unit, CHUNK // LANES)
        magnitude = [
            jnp.abs(
                tile[pl.ds(i * 256 + q * 16, 16), pl.ds(j * LANES, LANES)].astype(jnp.bfloat16)
                * scale
            )
            for q in range(16)
        ]
        current = magnitude
        for power in range(POWERS):
            total = tree_sum(current).astype(jnp.float32)
            acc[power, :, pl.ds(base + j * LANES, LANES)] += total[0:8] + total[8:16]
            if power < POWERS - 1:
                current = [a * b for a, b in zip(current, magnitude)]

    def advance(tile, item, done_tile, done_item):
        row = pl.multiple_of(ROWS + 8 * done_item[0], 8)
        lasts = []
        for share in range(SHARES):
            lasts.append(multiply(tile, item, share))
            accumulate(done_tile, done_item, share)
            if 0 < share < SHARES - 1:
                done_tile[pl.ds(row, 8), pl.ds(0, LANES)] = lasts[share - 1]

    def keep_self_apart(tile):
        block = tile[pl.ds(0, 2 * PIECE), pl.ds(0, 2 * PIECE)]
        same = lax.broadcasted_iota(jnp.int32, block.shape, 0) == lax.broadcasted_iota(
            jnp.int32, block.shape, 1
        )
        own = jnp.sum(jnp.where(same, block, 0.0), axis=0, keepdims=True)
        self_ref[...] = jnp.abs(own) * scale
        tile[pl.ds(0, 2 * PIECE), pl.ds(0, 2 * PIECE)] = jnp.where(same, 0.0, block)

    low_half = lax.broadcasted_iota(jnp.int32, (POWERS, 8, LANES), 2) < PIECE

    def sums_of(dx, dy):
        low, high = (
            acc[:, :, pl.ds(ROW[(dx, dy, half)] // LANES * LANES, LANES)] for half in (0, 1)
        )
        return jnp.sum(jnp.where(low_half, low, high), axis=1)

    def part_copy(n):
        dx, dy = PEERS[n]
        return remote(
            outgoing.at[n], incoming.at[n], part_send.at[n], part_recv.at[n], at(dx=dx, dy=dy)
        )

    def send_parts(before):
        for n in PART_SENDS[before]:
            outgoing[n] = sums_of(*PEERS[n])
            part_copy(n).start()

    def prepare(u):
        for n in range(0, len(ITEMS), 2):
            if n in BEFORE or n in PART_SENDS or n == OWN_ITEM + 1:

                @pl.when(u == n // 2)
                def _():
                    steps, rows = BEFORE.get(n, ([], []))
                    for step in steps:
                        communicate(step)
                    for step in rows:
                        partner_rows_ready(step)
                    if n == OWN_ITEM + 1:
                        keep_self_apart((tile_even, tile_odd)[OWN_ITEM % 2])
                    if n in PART_SENDS:
                        send_parts(n)

    communicate(0)
    tile_odd[...] = jnp.zeros_like(tile_odd)

    def body(u, carry):
        before, first, second = carry
        prepare(u)
        advance(tile_even, first, tile_odd, before)
        advance(tile_odd, second, tile_even, first)
        return second, item_at(2 * u + 2), item_at(2 * u + 3)

    lax.fori_loop(
        0, len(ITEMS) // 2, body, tuple(item_at(jnp.int32(n)) for n in (-1, 0, 1))
    )
    for unit in range(SHARES):
        accumulate(tile_odd, item_at(jnp.int32(len(ITEMS) - 1)), unit)
    send_parts(len(ITEMS) + 2)
    total = sums_of(0, 0)
    own = self_ref[...]
    powers = [own]
    for _ in range(POWERS - 1):
        powers.append(powers[-1] * own)
    total = total + jnp.concatenate(powers, axis=0)
    for n in range(len(PEERS)):
        part_copy(n).wait_recv()
        total = total + incoming[n]
    conn_ref[...] = total
    picked = jnp.concatenate([conn_ref[pl.ds(order_ref[t], 1), :] for t in range(POWERS)], axis=0)
    log_conn = jnp.log(picked)
    results[pl.ds(0, POWERS), :] = log_conn
    out_copies = [pltpu.make_async_copy(results.at[pl.ds(0, POWERS), :], log_conn_ref, out_sem.at[0])]
    out_copies[0].start()

    position = log_conn * ((BINS - 1) / log_total)
    position = jnp.concatenate(
        [position, jnp.zeros((LANES - POWERS, LANES), jnp.float32)], axis=0
    ).T
    levels = lax.broadcasted_iota(jnp.int32, (LANES, BINS), 1).astype(jnp.float32)
    for t in range(POWERS):
        weights = jnp.maximum(0.0, 1.0 - jnp.abs(position[:, t : t + 1] - levels))
        hist_ref[pl.ds(t, 1), :] = jnp.sum(weights, axis=0, keepdims=True)

    here = x * 4 + y

    def hist_copy(n, src):
        dx, dy = PEERS[n]
        return remote(
            hist_ref, plane_hist.at[src], hist_send.at[n], hist_recv.at[n], at(dx=dx, dy=dy)
        )

    for n in range(len(PEERS)):
        hist_copy(n, here).start()
    plane_hist[here] = hist_ref[...]
    for n in range(len(PEERS)):
        dx, dy = PEERS[n]
        hist_copy(n, lax.rem(x + (4 - dx), 4) * 4 + lax.rem(y + (4 - dy), 4)).wait_recv()
    plane_ref[...] = tree_sum([plane_hist[i] for i in range(16)])

    def line_copy(n, src):
        return remote(
            plane_ref, line_hist.at[src], line_send.at[n], line_recv.at[n], at(dz=LINE_PEERS[n])
        )

    for n in range(7):
        line_copy(n, z).start()
    line_hist[z] = plane_ref[...]
    for n in range(7):
        line_copy(n, lax.rem(z + (8 - LINE_PEERS[n]), 8)).wait_recv()
    line_ref[...] = tree_sum([line_hist[i] for i in range(8)])
    last = remote(line_ref, core_hist, last_send, last_recv, at(dc=1))
    last.start()
    last.wait_recv()
    hist = line_ref[...] + core_hist[...]

    hist = jnp.concatenate([hist, jnp.zeros((LANES - POWERS, BINS), jnp.float32)], axis=0).T
    centers = lax.broadcasted_iota(jnp.int32, hist.shape, 0).astype(jnp.float32) * (
        log_total / (BINS - 1)
    )

    def over_bins(value):
        return jnp.sum(value, axis=0, keepdims=True)

    weight_sum = over_bins(hist)
    ylog = jnp.log(hist + 1.0) - log_total
    xdev = centers - over_bins(hist * centers) / weight_sum
    ydev = ylog - over_bins(hist * ylog) / weight_sum
    sxx = jnp.maximum(over_bins(hist * xdev * xdev) / weight_sum, 0.05)
    syy = jnp.maximum(over_bins(hist * ydev * ydev) / weight_sum, 0.05)
    sxy = over_bins(hist * xdev * ydev) / weight_sum
    fit_out[...] = (-sxy * jnp.abs(sxy) / (sxx * syy))[:, :POWERS]
    slope_out[...] = (sxy / sxx)[:, :POWERS]
    out_copies.append(pltpu.make_async_copy(fit_out, fit_ref, out_sem.at[1]))
    out_copies.append(pltpu.make_async_copy(slope_out, slope_ref, out_sem.at[2]))
    for copy in out_copies[1:]:
        copy.start()
    for sends in PLANE_SENDS:
        for send in sends:
            plane_copy(*send).wait_send()
    for step in range(1, Z_STEPS + 1):
        for direction in (1, -1):
            z_copy(direction, step).wait_send()
    for step in range(Z_STEPS + 1):
        core_copy(step).wait_send()
    for n in range(len(PEERS)):
        part_copy(n).wait_send()
        hist_copy(n, here).wait_send()
    for n in range(7):
        line_copy(n, z).wait_send()
    last.wait_send()
    for copy in out_copies:
        copy.wait()


def on_device(expression, power_order):
    genes_dev, samples = expression.shape
    powers = power_order.shape[0]
    total_genes = genes_dev * lax.axis_size(AXES)
    plane, line = len(PEERS), 7
    dma = pltpu.SemaphoreType.DMA
    log_conn, fit, slope = pl.pallas_call(
        functools.partial(kernel, math.log(total_genes), samples),
        out_shape=(
            jax.ShapeDtypeStruct((powers, genes_dev), jnp.float32),
            jax.ShapeDtypeStruct((1, powers), jnp.float32),
            jax.ShapeDtypeStruct((1, powers), jnp.float32),
        ),
        in_specs=[pl.BlockSpec(memory_space=pltpu.HBM), pl.BlockSpec(memory_space=pltpu.SMEM)],
        out_specs=(pl.BlockSpec(memory_space=pltpu.HBM),) * 3,
        scratch_shapes=[
            pltpu.VMEM((SLABS, 2048, LANES), jnp.bfloat16),
            pltpu.VMEM((SLABS, 2048, LANES), jnp.bfloat16),
            pltpu.VMEM((POWERS, 8, 2048), jnp.float32),
            pltpu.VMEM((ROWS + 8 * STEPS, CHUNK), jnp.float32),
            pltpu.VMEM((ROWS + 8 * STEPS, CHUNK), jnp.float32),
            pltpu.VMEM((1, LANES), jnp.float32),
            pltpu.VMEM((plane, powers, LANES), jnp.float32),
            pltpu.VMEM((plane, powers, LANES), jnp.float32),
            pltpu.VMEM((powers, LANES), jnp.float32),
            pltpu.VMEM((powers, BINS), jnp.float32),
            pltpu.VMEM((powers, BINS), jnp.float32),
            pltpu.VMEM((16, powers, BINS), jnp.float32),
            pltpu.VMEM((8, powers, BINS), jnp.float32),
            pltpu.VMEM((powers, BINS), jnp.float32),
            pltpu.VMEM((powers, BINS), jnp.float32),
            pltpu.VMEM((powers, LANES), jnp.float32),
            pltpu.VMEM((1, powers), jnp.float32),
            pltpu.VMEM((1, powers), jnp.float32),
            dma((2, SLABS)),
            dma((4, STEPS)),
            dma((4, STEPS)),
            dma((2, Z_STEPS)),
            dma((2, Z_STEPS)),
            dma((STEPS,)),
            dma((STEPS,)),
            dma((plane,)),
            dma((plane,)),
            dma((plane,)),
            dma((plane,)),
            dma((line,)),
            dma((line,)),
            dma,
            dma,
            dma((3,)),
        ],
        compiler_params=pltpu.CompilerParams(
            collective_id=0, has_side_effects=True, vmem_limit_bytes=66_800_000
        ),
        name="coexpression",
    )(expression, power_order)
    return log_conn.T, fit.reshape(powers), slope.reshape(powers)


def solution(mesh):
    torus = Mesh(mesh.devices.reshape(8, 4, 4, 2), AXES)
    along = P(AXES, None)
    return jax.shard_map(
        on_device,
        mesh=torus,
        in_specs=(along, P()),
        out_specs=(along, P(), P()),
        check_vma=False,
    )
```

```python
import functools
import math

import jax
import jax.numpy as jnp
from jax import lax
from jax.experimental import pallas as pl
from jax.experimental.pallas import tpu as pltpu
from jax.sharding import Mesh
from jax.sharding import PartitionSpec as P

AXES = ("row_0", "row_1", "col_0", "col_1")
POWERS = 20
BINS = 128
LANES = 128
SLABS = 8
PIECE = 64
CHUNK = 256
STEPS = 8
SHARES = 4
MESH_ID = pl.DeviceIdType.MESH


def wrap4(d):
    return {0: 0, 1: 1, 2: 2, 3: -1}[d % 4]


X_UP = [(1, 0, 0), (1, 0, 1), (2, 0, 0), (1, 1, 1), (1, -1, 1), (2, 0, 1), (1, 2, 1)]
X_DOWN = [(-1, 0, 0), (-1, 0, 1), (-1, 1, 1), (-1, -1, 1), (-1, 2, 1), (2, 1, 1), (2, -1, 1), (2, 2, 1)]


def mirrored(order):
    return [(dy, dx, 1 - half) for dx, dy, half in order]


ARRIVALS = {
    (1, 0): X_UP,
    (-1, 0): X_DOWN,
    (0, 1): mirrored(X_UP),
    (0, -1): mirrored(X_DOWN),
}
LINKS = list(ARRIVALS)


def place_pieces():
    row, step_of = {}, {(0, 0, 0): 0, (0, 0, 1): 0}
    for step in range(1, STEPS + 1):
        free = {0: [0, 2], 1: [1, 3]}
        here = [order[step - 1] for order in ARRIVALS.values() if step <= len(order)]
        if step == STEPS:
            here = [(0, 0, 0), (0, 0, 1)] + here
        for piece in here:
            slot = free[piece[2]].pop(0)
            row[piece] = (step - 1) * CHUNK + slot * PIECE
            step_of.setdefault(piece, step)
    return row, step_of


ROW, STEP_OF = place_pieces()


def sends_by_step():
    out = [[] for _ in range(STEPS + 1)]
    for k, (lx, ly) in enumerate(LINKS):
        for i, (dx, dy, half) in enumerate(ARRIVALS[(lx, ly)]):
            mine = (wrap4(dx - lx), wrap4(dy - ly), half)
            out[STEP_OF[mine]].append((k, i, ROW[mine], ROW[(dx, dy, half)]))
    return out


PLANE_SENDS = sends_by_step()
PEERS = sorted(
    [(dx, dy) for dx in (0, 1, -1, 2) for dy in (0, 1, -1, 2) if (dx, dy) != (0, 0)],
    key=lambda peer: -abs(peer[0]) - abs(peer[1]),
)
LINE_PEERS = (4, 3, 5, 2, 6, 1, 7)
Z_STEPS = 7
ROWS = 512
ITEMS = (
    [(0, 0), (1, 0), (2, 0), (0, 1), (1, 1), (2, 1), (3, 0), (3, 1), (4, 0), (4, 1)]
    + [(c, 2) for c in range(5)]
    + [(5, 0), (5, 1), (5, 2), (6, 0), (6, 1), (6, 2), (6, 3), (5, 3), (4, 3)]
    + [(7, 1), (7, 0), (7, 2), (7, 3), (3, 3), (2, 3), (1, 3), (0, 3)]
)
BEFORE = {
    0: ([1, 2], [0, 1]),
    2: ([3], [2, 3]),
    6: ([4], []),
    8: ([5], []),
    10: ([], [4, 5]),
    14: ([6], []),
    18: ([7], []),
    20: ([], [6, 7]),
    24: ([8], []),
}
OWN_ITEM = ITEMS.index((STEPS - 1, 0))


def item_at(n):
    chunk, block = jnp.int32(0), jnp.int32(0)
    for k, (c, b) in enumerate(ITEMS):
        chunk = jnp.where(n == k, c, chunk)
        block = jnp.where(n == k, b, block)
    return chunk, block


def sends_before():
    bounds = [28, 30, len(ITEMS) + 2]
    out = {n: [] for n in bounds}
    for peer, (dx, dy) in enumerate(PEERS):
        chunks = [ROW[(dx, dy, half)] // CHUNK for half in (0, 1)]
        done = max(n for n, (chunk, _) in enumerate(ITEMS) if chunk in chunks)
        out[min(n for n in bounds if n - 2 >= done)].append(peer)
    return out


PART_SENDS = sends_before()


def tree_sum(values):
    while len(values) > 1:
        pairs = [a + b for a, b in zip(values[::2], values[1::2])]
        values = pairs + ([values[-1]] if len(values) % 2 else [])
    return values[0]


def kernel(
    log_total,
    samples,
    x_ref,
    order_ref,
    log_conn_ref,
    fit_ref,
    slope_ref,
    genes,
    partners,
    acc,
    tile_even,
    tile_odd,
    self_ref,
    outgoing,
    incoming,
    conn_ref,
    hist_ref,
    plane_ref,
    plane_hist,
    line_hist,
    core_hist,
    line_ref,
    results,
    fit_out,
    slope_out,
    local_sem,
    plane_send,
    plane_recv,
    z_send,
    z_recv,
    core_send,
    core_recv,
    part_send,
    part_recv,
    hist_send,
    hist_recv,
    line_send,
    line_recv,
    last_send,
    last_recv,
    out_sem,
):
    z, y, x, core = (lax.axis_index(a) for a in AXES)

    def at(dx=0, dy=0, dz=0, dc=0):
        return (
            lax.rem(z + (dz + 8), 8),
            lax.rem(y + (dy + 4), 4),
            lax.rem(x + (dx + 4), 4),
            lax.rem(core + dc, 2),
        )

    own_row = ROW[(0, 0, 0)]
    loads = []
    for k in range(SLABS):
        cols = pl.ds(k * LANES, LANES)
        loads.append(
            pltpu.make_async_copy(
                x_ref.at[:, cols], genes.at[k, pl.ds(own_row, 2 * PIECE), :], local_sem.at[0, k]
            )
        )
        loads.append(
            pltpu.make_async_copy(
                x_ref.at[:, cols], partners.at[k, pl.ds(0, 2 * PIECE), :], local_sem.at[1, k]
            )
        )
    for copy in loads:
        copy.start()

    barrier = pltpu.get_barrier_semaphore()
    near = [at(dx=1), at(dx=-1), at(dy=1), at(dy=-1), at(dz=1), at(dz=-1), at(dc=1)]
    for device in near:
        pl.semaphore_signal(barrier, inc=1, device_id=device, device_id_type=MESH_ID)
    acc[...] = jnp.zeros_like(acc)
    for copy in loads:
        copy.wait()
    pl.semaphore_wait(barrier, len(near))

    def remote(src, dst, send_sem, recv_sem, device):
        return pltpu.make_async_remote_copy(
            src_ref=src,
            dst_ref=dst,
            send_sem=send_sem,
            recv_sem=recv_sem,
            device_id=device,
            device_id_type=MESH_ID,
        )

    def plane_copy(k, i, src, dst):
        lx, ly = LINKS[k]
        return remote(
            genes.at[:, pl.ds(src, PIECE), :],
            genes.at[:, pl.ds(dst, PIECE), :],
            plane_send.at[k, i],
            plane_recv.at[k, i],
            at(dx=-lx, dy=-ly),
        )

    def z_row(direction, step):
        return step * CHUNK + (0 if direction == 1 else PIECE)

    def z_copy(direction, step):
        if step <= 2:
            first = step == 1
            src = 0 if first == (direction == 1) else PIECE
        else:
            src = z_row(direction, step - 2)
        side = 0 if direction == 1 else 1
        return remote(
            partners.at[:, pl.ds(src, PIECE), :],
            partners.at[:, pl.ds(z_row(direction, step), PIECE), :],
            z_send.at[side, step - 1],
            z_recv.at[side, step - 1],
            at(dz=-direction),
        )

    def core_copy(step):
        return remote(
            partners.at[:, pl.ds(step * CHUNK, 2 * PIECE), :],
            partners.at[:, pl.ds(step * CHUNK + 2 * PIECE, 2 * PIECE), :],
            core_send.at[step],
            core_recv.at[step],
            at(dc=1),
        )

    def communicate(step):
        if step:
            for k, link in enumerate(LINKS):
                if step <= len(ARRIVALS[link]):
                    plane_copy(k, step - 1, 0, ROW[ARRIVALS[link][step - 1]]).wait_recv()
            if step <= Z_STEPS:
                for direction in (1, -1):
                    z_copy(direction, step).wait_recv()
        for send in PLANE_SENDS[step]:
            plane_copy(*send).start()
        for later in (1, 2) if step == 0 else (step + 2,):
            if later <= Z_STEPS:
                for direction in (1, -1):
                    z_copy(direction, later).start()
        if step <= Z_STEPS:
            core_copy(step).start()

    def partner_rows_ready(step):
        core_copy(step).wait_recv()

    def lanes_of(ref, first, count, part):
        slabs = range(part * SLABS // SHARES, (part + 1) * SLABS // SHARES)
        return jnp.concatenate(
            [ref[k, pl.ds(pl.multiple_of(first, PIECE), count), :] for k in slabs], axis=1
        )

    scale = 1.0 / samples

    def multiply(tile, item, part):
        chunk, block = item
        product = lax.dot_general(
            lanes_of(partners, block * ROWS, ROWS, part),
            lanes_of(genes, chunk * CHUNK, CHUNK, part),
            (((1,), (1,)), ((), ())),
            preferred_element_type=jnp.float32,
        )
        if part == 0:
            tile[pl.ds(0, ROWS), :] = product
        else:
            tile[pl.ds(0, ROWS), :] += product
        return product[ROWS - 8 :, :LANES]

    def accumulate(tile, item, unit):
        base = pl.multiple_of(item[0] * CHUNK, CHUNK)
        i, j = divmod(unit, CHUNK // LANES)
        magnitude = [
            jnp.abs(
                tile[pl.ds(i * 256 + q * 16, 16), pl.ds(j * LANES, LANES)].astype(jnp.bfloat16)
                * scale
            )
            for q in range(16)
        ]
        current = magnitude
        for power in range(POWERS):
            total = tree_sum(current).astype(jnp.float32)
            acc[power, :, pl.ds(base + j * LANES, LANES)] += total[0:8] + total[8:16]
            if power < POWERS - 1:
                current = [a * b for a, b in zip(current, magnitude)]

    def advance(tile, item, done_tile, done_item):
        row = pl.multiple_of(ROWS + 8 * done_item[0], 8)
        lasts = []
        for share in range(SHARES):
            lasts.append(multiply(tile, item, share))
            accumulate(done_tile, done_item, share)
            if share == 0:
                done_tile[pl.ds(row, 8), pl.ds(0, LANES)] = lasts[0]
            if share == SHARES - 2:
                done_tile[pl.ds(row, 8), pl.ds(0, LANES)] = lasts[1]

    def keep_self_apart(tile):
        block = tile[pl.ds(0, 2 * PIECE), pl.ds(0, 2 * PIECE)]
        same = lax.broadcasted_iota(jnp.int32, block.shape, 0) == lax.broadcasted_iota(
            jnp.int32, block.shape, 1
        )
        own = jnp.sum(jnp.where(same, block, 0.0), axis=0, keepdims=True)
        self_ref[...] = jnp.abs(own) * scale
        tile[pl.ds(0, 2 * PIECE), pl.ds(0, 2 * PIECE)] = jnp.where(same, 0.0, block)

    low_half = lax.broadcasted_iota(jnp.int32, (POWERS, 8, LANES), 2) < PIECE

    def sums_of(dx, dy):
        low, high = (
            acc[:, :, pl.ds(ROW[(dx, dy, half)] // LANES * LANES, LANES)] for half in (0, 1)
        )
        return jnp.sum(jnp.where(low_half, low, high), axis=1)

    def part_copy(n):
        dx, dy = PEERS[n]
        return remote(
            outgoing.at[n], incoming.at[n], part_send.at[n], part_recv.at[n], at(dx=dx, dy=dy)
        )

    def send_parts(before):
        for n in PART_SENDS[before]:
            outgoing[n] = sums_of(*PEERS[n])
            part_copy(n).start()

    def prepare(u):
        for n in range(0, len(ITEMS), 2):
            if n in BEFORE or n in PART_SENDS or n == OWN_ITEM + 1:

                @pl.when(u == n // 2)
                def _():
                    steps, rows = BEFORE.get(n, ([], []))
                    for step in steps:
                        communicate(step)
                    for step in rows:
                        partner_rows_ready(step)
                    if n == OWN_ITEM + 1:
                        keep_self_apart((tile_even, tile_odd)[OWN_ITEM % 2])
                    if n in PART_SENDS:
                        send_parts(n)

    communicate(0)
    tile_odd[...] = jnp.zeros_like(tile_odd)

    def body(u, carry):
        before, first, second = carry
        prepare(u)
        advance(tile_even, first, tile_odd, before)
        advance(tile_odd, second, tile_even, first)
        return second, item_at(2 * u + 2), item_at(2 * u + 3)

    lax.fori_loop(
        0, len(ITEMS) // 2, body, tuple(item_at(jnp.int32(n)) for n in (-1, 0, 1))
    )
    for unit in range(SHARES):
        accumulate(tile_odd, item_at(jnp.int32(len(ITEMS) - 1)), unit)
    send_parts(len(ITEMS) + 2)
    total = sums_of(0, 0)
    own = self_ref[...]
    powers = [own]
    for _ in range(POWERS - 1):
        powers.append(powers[-1] * own)
    total = total + jnp.concatenate(powers, axis=0)
    for n in range(len(PEERS)):
        part_copy(n).wait_recv()
        total = total + incoming[n]
    conn_ref[...] = total
    picked = jnp.concatenate([conn_ref[pl.ds(order_ref[t], 1), :] for t in range(POWERS)], axis=0)
    log_conn = jnp.log(picked)
    results[pl.ds(0, POWERS), :] = log_conn
    out_copies = [pltpu.make_async_copy(results.at[pl.ds(0, POWERS), :], log_conn_ref, out_sem.at[0])]
    out_copies[0].start()

    position = log_conn * ((BINS - 1) / log_total)
    position = jnp.concatenate(
        [position, jnp.zeros((LANES - POWERS, LANES), jnp.float32)], axis=0
    ).T
    levels = lax.broadcasted_iota(jnp.int32, (LANES, BINS), 1).astype(jnp.float32)
    for t in range(POWERS):
        weights = jnp.maximum(0.0, 1.0 - jnp.abs(position[:, t : t + 1] - levels))
        hist_ref[pl.ds(t, 1), :] = jnp.sum(weights, axis=0, keepdims=True)

    here = x * 4 + y

    def hist_copy(n, src):
        dx, dy = PEERS[n]
        return remote(
            hist_ref, plane_hist.at[src], hist_send.at[n], hist_recv.at[n], at(dx=dx, dy=dy)
        )

    for n in range(len(PEERS)):
        hist_copy(n, here).start()
    plane_hist[here] = hist_ref[...]
    for n in range(len(PEERS)):
        dx, dy = PEERS[n]
        hist_copy(n, lax.rem(x + (4 - dx), 4) * 4 + lax.rem(y + (4 - dy), 4)).wait_recv()
    plane_ref[...] = tree_sum([plane_hist[i] for i in range(16)])

    def line_copy(n, src):
        return remote(
            plane_ref, line_hist.at[src], line_send.at[n], line_recv.at[n], at(dz=LINE_PEERS[n])
        )

    for n in range(7):
        line_copy(n, z).start()
    line_hist[z] = plane_ref[...]
    for n in range(7):
        line_copy(n, lax.rem(z + (8 - LINE_PEERS[n]), 8)).wait_recv()
    line_ref[...] = tree_sum([line_hist[i] for i in range(8)])
    last = remote(line_ref, core_hist, last_send, last_recv, at(dc=1))
    last.start()
    last.wait_recv()
    hist = line_ref[...] + core_hist[...]

    hist = jnp.concatenate([hist, jnp.zeros((LANES - POWERS, BINS), jnp.float32)], axis=0).T
    centers = lax.broadcasted_iota(jnp.int32, hist.shape, 0).astype(jnp.float32) * (
        log_total / (BINS - 1)
    )

    def over_bins(value):
        return jnp.sum(value, axis=0, keepdims=True)

    weight_sum = over_bins(hist)
    ylog = jnp.log(hist + 1.0) - log_total
    xdev = centers - over_bins(hist * centers) / weight_sum
    ydev = ylog - over_bins(hist * ylog) / weight_sum
    sxx = jnp.maximum(over_bins(hist * xdev * xdev) / weight_sum, 0.05)
    syy = jnp.maximum(over_bins(hist * ydev * ydev) / weight_sum, 0.05)
    sxy = over_bins(hist * xdev * ydev) / weight_sum
    fit_out[...] = (-sxy * jnp.abs(sxy) / (sxx * syy))[:, :POWERS]
    slope_out[...] = (sxy / sxx)[:, :POWERS]
    out_copies.append(pltpu.make_async_copy(fit_out, fit_ref, out_sem.at[1]))
    out_copies.append(pltpu.make_async_copy(slope_out, slope_ref, out_sem.at[2]))
    for copy in out_copies[1:]:
        copy.start()
    for sends in PLANE_SENDS:
        for send in sends:
            plane_copy(*send).wait_send()
    for step in range(1, Z_STEPS + 1):
        for direction in (1, -1):
            z_copy(direction, step).wait_send()
    for step in range(Z_STEPS + 1):
        core_copy(step).wait_send()
    for n in range(len(PEERS)):
        part_copy(n).wait_send()
        hist_copy(n, here).wait_send()
    for n in range(7):
        line_copy(n, z).wait_send()
    last.wait_send()
    for copy in out_copies:
        copy.wait()


def on_device(expression, power_order):
    genes_dev, samples = expression.shape
    powers = power_order.shape[0]
    total_genes = genes_dev * lax.axis_size(AXES)
    plane, line = len(PEERS), 7
    dma = pltpu.SemaphoreType.DMA
    log_conn, fit, slope = pl.pallas_call(
        functools.partial(kernel, math.log(total_genes), samples),
        out_shape=(
            jax.ShapeDtypeStruct((powers, genes_dev), jnp.float32),
            jax.ShapeDtypeStruct((1, powers), jnp.float32),
            jax.ShapeDtypeStruct((1, powers), jnp.float32),
        ),
        in_specs=[pl.BlockSpec(memory_space=pltpu.HBM), pl.BlockSpec(memory_space=pltpu.SMEM)],
        out_specs=(pl.BlockSpec(memory_space=pltpu.HBM),) * 3,
        scratch_shapes=[
            pltpu.VMEM((SLABS, 2048, LANES), jnp.bfloat16),
            pltpu.VMEM((SLABS, 2048, LANES), jnp.bfloat16),
            pltpu.VMEM((POWERS, 8, 2048), jnp.float32),
            pltpu.VMEM((ROWS + 8 * STEPS, CHUNK), jnp.float32),
            pltpu.VMEM((ROWS + 8 * STEPS, CHUNK), jnp.float32),
            pltpu.VMEM((1, LANES), jnp.float32),
            pltpu.VMEM((plane, powers, LANES), jnp.float32),
            pltpu.VMEM((plane, powers, LANES), jnp.float32),
            pltpu.VMEM((powers, LANES), jnp.float32),
            pltpu.VMEM((powers, BINS), jnp.float32),
            pltpu.VMEM((powers, BINS), jnp.float32),
            pltpu.VMEM((16, powers, BINS), jnp.float32),
            pltpu.VMEM((8, powers, BINS), jnp.float32),
            pltpu.VMEM((powers, BINS), jnp.float32),
            pltpu.VMEM((powers, BINS), jnp.float32),
            pltpu.VMEM((powers, LANES), jnp.float32),
            pltpu.VMEM((1, powers), jnp.float32),
            pltpu.VMEM((1, powers), jnp.float32),
            dma((2, SLABS)),
            dma((4, STEPS)),
            dma((4, STEPS)),
            dma((2, Z_STEPS)),
            dma((2, Z_STEPS)),
            dma((STEPS,)),
            dma((STEPS,)),
            dma((plane,)),
            dma((plane,)),
            dma((plane,)),
            dma((plane,)),
            dma((line,)),
            dma((line,)),
            dma,
            dma,
            dma((3,)),
        ],
        compiler_params=pltpu.CompilerParams(
            collective_id=0, has_side_effects=True, vmem_limit_bytes=66_800_000
        ),
        name="coexpression",
    )(expression, power_order)
    return log_conn.T, fit.reshape(powers), slope.reshape(powers)


def solution(mesh):
    torus = Mesh(mesh.devices.reshape(8, 4, 4, 2), AXES)
    along = P(AXES, None)
    return jax.shard_map(
        on_device,
        mesh=torus,
        in_specs=(along, P()),
        out_specs=(along, P(), P()),
        check_vma=False,
    )
```

```python
import functools
import math

import jax
import jax.numpy as jnp
from jax import lax
from jax.experimental import pallas as pl
from jax.experimental.pallas import tpu as pltpu
from jax.sharding import Mesh
from jax.sharding import PartitionSpec as P

AXES = ("row_0", "row_1", "col_0", "col_1")
POWERS = 20
BINS = 128
LANES = 128
SLABS = 8
PIECE = 64
CHUNK = 256
STEPS = 8
SHARES = 4
MESH_ID = pl.DeviceIdType.MESH


def wrap4(d):
    return {0: 0, 1: 1, 2: 2, 3: -1}[d % 4]


X_UP = [(1, 0, 0), (1, 0, 1), (2, 0, 0), (1, 1, 1), (1, -1, 1), (2, 0, 1), (1, 2, 1)]
X_DOWN = [(-1, 0, 0), (-1, 0, 1), (-1, 1, 1), (-1, -1, 1), (-1, 2, 1), (2, 1, 1), (2, -1, 1), (2, 2, 1)]


def mirrored(order):
    return [(dy, dx, 1 - half) for dx, dy, half in order]


ARRIVALS = {
    (1, 0): X_UP,
    (-1, 0): X_DOWN,
    (0, 1): mirrored(X_UP),
    (0, -1): mirrored(X_DOWN),
}
LINKS = list(ARRIVALS)


def place_pieces():
    row, step_of = {}, {(0, 0, 0): 0, (0, 0, 1): 0}
    for step in range(1, STEPS + 1):
        free = {0: [0, 2], 1: [1, 3]}
        here = [order[step - 1] for order in ARRIVALS.values() if step <= len(order)]
        if step == STEPS:
            here = [(0, 0, 0), (0, 0, 1)] + here
        for piece in here:
            slot = free[piece[2]].pop(0)
            row[piece] = (step - 1) * CHUNK + slot * PIECE
            step_of.setdefault(piece, step)
    return row, step_of


ROW, STEP_OF = place_pieces()


def sends_by_step():
    out = [[] for _ in range(STEPS + 1)]
    for k, (lx, ly) in enumerate(LINKS):
        for i, (dx, dy, half) in enumerate(ARRIVALS[(lx, ly)]):
            mine = (wrap4(dx - lx), wrap4(dy - ly), half)
            out[STEP_OF[mine]].append((k, i, ROW[mine], ROW[(dx, dy, half)]))
    return out


PLANE_SENDS = sends_by_step()
PEERS = sorted(
    [(dx, dy) for dx in (0, 1, -1, 2) for dy in (0, 1, -1, 2) if (dx, dy) != (0, 0)],
    key=lambda peer: -abs(peer[0]) - abs(peer[1]),
)
LINE_PEERS = (4, 3, 5, 2, 6, 1, 7)
Z_STEPS = 7
ROWS = 512
ITEMS = (
    [(0, 0), (1, 0), (2, 0), (0, 1), (1, 1), (2, 1), (3, 0), (3, 1), (4, 0), (4, 1)]
    + [(c, 2) for c in range(5)]
    + [(5, 0), (5, 1), (5, 2), (6, 0), (6, 1), (6, 2), (6, 3), (5, 3), (4, 3)]
    + [(7, 1), (7, 0), (7, 2), (7, 3), (3, 3), (2, 3), (1, 3), (0, 3)]
)
BEFORE = {
    0: ([1, 2], [0, 1]),
    2: ([3], [2, 3]),
    6: ([4], []),
    8: ([5], []),
    10: ([], [4, 5]),
    14: ([6], []),
    18: ([7], []),
    20: ([], [6, 7]),
    24: ([8], []),
}
OWN_ITEM = ITEMS.index((STEPS - 1, 0))


def item_at(n):
    chunk, block = jnp.int32(0), jnp.int32(0)
    for k, (c, b) in enumerate(ITEMS):
        chunk = jnp.where(n == k, c, chunk)
        block = jnp.where(n == k, b, block)
    return chunk, block


def sends_before():
    bounds = [28, 30, len(ITEMS) + 2]
    out = {n: [] for n in bounds}
    for peer, (dx, dy) in enumerate(PEERS):
        chunks = [ROW[(dx, dy, half)] // CHUNK for half in (0, 1)]
        done = max(n for n, (chunk, _) in enumerate(ITEMS) if chunk in chunks)
        out[min(n for n in bounds if n - 2 >= done)].append(peer)
    return out


PART_SENDS = sends_before()


def tree_sum(values):
    while len(values) > 1:
        pairs = [a + b for a, b in zip(values[::2], values[1::2])]
        values = pairs + ([values[-1]] if len(values) % 2 else [])
    return values[0]


def kernel(
    log_total,
    samples,
    x_ref,
    order_ref,
    log_conn_ref,
    fit_ref,
    slope_ref,
    genes,
    partners,
    acc,
    tile_even,
    tile_odd,
    self_ref,
    outgoing,
    incoming,
    conn_ref,
    hist_ref,
    plane_ref,
    plane_hist,
    line_hist,
    core_hist,
    line_ref,
    results,
    fit_out,
    slope_out,
    local_sem,
    plane_send,
    plane_recv,
    z_send,
    z_recv,
    core_send,
    core_recv,
    part_send,
    part_recv,
    hist_send,
    hist_recv,
    line_send,
    line_recv,
    last_send,
    last_recv,
    out_sem,
):
    z, y, x, core = (lax.axis_index(a) for a in AXES)

    def at(dx=0, dy=0, dz=0, dc=0):
        return (
            lax.rem(z + (dz + 8), 8),
            lax.rem(y + (dy + 4), 4),
            lax.rem(x + (dx + 4), 4),
            lax.rem(core + dc, 2),
        )

    own_row = ROW[(0, 0, 0)]
    loads = []
    for k in range(SLABS):
        cols = pl.ds(k * LANES, LANES)
        loads.append(
            pltpu.make_async_copy(
                x_ref.at[:, cols], genes.at[k, pl.ds(own_row, 2 * PIECE), :], local_sem.at[0, k]
            )
        )
        loads.append(
            pltpu.make_async_copy(
                x_ref.at[:, cols], partners.at[k, pl.ds(0, 2 * PIECE), :], local_sem.at[1, k]
            )
        )
    for copy in loads[::2] + loads[1::2]:
        copy.start()

    barrier = pltpu.get_barrier_semaphore()
    near = [at(dx=1), at(dx=-1), at(dy=1), at(dy=-1), at(dz=1), at(dz=-1), at(dc=1)]
    for device in near:
        pl.semaphore_signal(barrier, inc=1, device_id=device, device_id_type=MESH_ID)
    acc[...] = jnp.zeros_like(acc)
    for copy in loads[::2]:
        copy.wait()
    pl.semaphore_wait(barrier, len(near))

    def remote(src, dst, send_sem, recv_sem, device):
        return pltpu.make_async_remote_copy(
            src_ref=src,
            dst_ref=dst,
            send_sem=send_sem,
            recv_sem=recv_sem,
            device_id=device,
            device_id_type=MESH_ID,
        )

    def plane_copy(k, i, src, dst):
        lx, ly = LINKS[k]
        return remote(
            genes.at[:, pl.ds(src, PIECE), :],
            genes.at[:, pl.ds(dst, PIECE), :],
            plane_send.at[k, i],
            plane_recv.at[k, i],
            at(dx=-lx, dy=-ly),
        )

    def z_row(direction, step):
        return step * CHUNK + (0 if direction == 1 else PIECE)

    def z_copy(direction, step):
        if step <= 2:
            first = step == 1
            src = 0 if first == (direction == 1) else PIECE
        else:
            src = z_row(direction, step - 2)
        side = 0 if direction == 1 else 1
        return remote(
            partners.at[:, pl.ds(src, PIECE), :],
            partners.at[:, pl.ds(z_row(direction, step), PIECE), :],
            z_send.at[side, step - 1],
            z_recv.at[side, step - 1],
            at(dz=-direction),
        )

    def core_copy(step):
        return remote(
            partners.at[:, pl.ds(step * CHUNK, 2 * PIECE), :],
            partners.at[:, pl.ds(step * CHUNK + 2 * PIECE, 2 * PIECE), :],
            core_send.at[step],
            core_recv.at[step],
            at(dc=1),
        )

    def communicate(step):
        if step:
            for k, link in enumerate(LINKS):
                if step <= len(ARRIVALS[link]):
                    plane_copy(k, step - 1, 0, ROW[ARRIVALS[link][step - 1]]).wait_recv()
            if step <= Z_STEPS:
                for direction in (1, -1):
                    z_copy(direction, step).wait_recv()
        for send in PLANE_SENDS[step]:
            plane_copy(*send).start()
        if step == 0:
            for copy in loads[1::2]:
                copy.wait()
        for later in (1, 2) if step == 0 else (step + 2,):
            if later <= Z_STEPS:
                for direction in (1, -1):
                    z_copy(direction, later).start()
        if step <= Z_STEPS:
            core_copy(step).start()

    def partner_rows_ready(step):
        core_copy(step).wait_recv()

    def lanes_of(ref, first, count, part):
        slabs = range(part * SLABS // SHARES, (part + 1) * SLABS // SHARES)
        return jnp.concatenate(
            [ref[k, pl.ds(pl.multiple_of(first, PIECE), count), :] for k in slabs], axis=1
        )

    scale = 1.0 / samples

    def multiply(tile, item, part):
        chunk, block = item
        product = lax.dot_general(
            lanes_of(partners, block * ROWS, ROWS, part),
            lanes_of(genes, chunk * CHUNK, CHUNK, part),
            (((1,), (1,)), ((), ())),
            preferred_element_type=jnp.float32,
        )
        if part == 0:
            tile[pl.ds(0, ROWS), :] = product
        else:
            tile[pl.ds(0, ROWS), :] += product
        return product[ROWS - 8 :, :LANES]

    def accumulate(tile, item, unit):
        base = pl.multiple_of(item[0] * CHUNK, CHUNK)
        i, j = divmod(unit, CHUNK // LANES)
        magnitude = [
            jnp.abs(
                tile[pl.ds(i * 256 + q * 16, 16), pl.ds(j * LANES, LANES)].astype(jnp.bfloat16)
                * scale
            )
            for q in range(16)
        ]
        current = magnitude
        for power in range(POWERS):
            total = tree_sum(current).astype(jnp.float32)
            acc[power, :, pl.ds(base + j * LANES, LANES)] += total[0:8] + total[8:16]
            if power < POWERS - 1:
                current = [a * b for a, b in zip(current, magnitude)]

    def advance(tile, item, done_tile, done_item):
        row = pl.multiple_of(ROWS + 8 * done_item[0], 8)
        lasts = []
        for share in range(SHARES):
            lasts.append(multiply(tile, item, share))
            accumulate(done_tile, done_item, share)
            if share == 0:
                done_tile[pl.ds(row, 8), pl.ds(0, LANES)] = lasts[0]
            if share == SHARES - 2:
                done_tile[pl.ds(row, 8), pl.ds(0, LANES)] = lasts[1]

    def keep_self_apart(tile):
        block = tile[pl.ds(0, 2 * PIECE), pl.ds(0, 2 * PIECE)]
        same = lax.broadcasted_iota(jnp.int32, block.shape, 0) == lax.broadcasted_iota(
            jnp.int32, block.shape, 1
        )
        own = jnp.sum(jnp.where(same, block, 0.0), axis=0, keepdims=True)
        self_ref[...] = jnp.abs(own) * scale
        tile[pl.ds(0, 2 * PIECE), pl.ds(0, 2 * PIECE)] = jnp.where(same, 0.0, block)

    low_half = lax.broadcasted_iota(jnp.int32, (POWERS, 8, LANES), 2) < PIECE

    def sums_of(dx, dy):
        low, high = (
            acc[:, :, pl.ds(ROW[(dx, dy, half)] // LANES * LANES, LANES)] for half in (0, 1)
        )
        return jnp.sum(jnp.where(low_half, low, high), axis=1)

    def part_copy(n):
        dx, dy = PEERS[n]
        return remote(
            outgoing.at[n], incoming.at[n], part_send.at[n], part_recv.at[n], at(dx=dx, dy=dy)
        )

    def send_parts(before):
        for n in PART_SENDS[before]:
            outgoing[n] = sums_of(*PEERS[n])
            part_copy(n).start()

    def prepare(u):
        for n in range(0, len(ITEMS), 2):
            if n in BEFORE or n in PART_SENDS or n == OWN_ITEM + 1:

                @pl.when(u == n // 2)
                def _():
                    steps, rows = BEFORE.get(n, ([], []))
                    for step in steps:
                        communicate(step)
                    for step in rows:
                        partner_rows_ready(step)
                    if n == OWN_ITEM + 1:
                        keep_self_apart((tile_even, tile_odd)[OWN_ITEM % 2])
                    if n in PART_SENDS:
                        send_parts(n)

    communicate(0)
    tile_odd[...] = jnp.zeros_like(tile_odd)

    def body(u, carry):
        before, first, second = carry
        prepare(u)
        advance(tile_even, first, tile_odd, before)
        advance(tile_odd, second, tile_even, first)
        return second, item_at(2 * u + 2), item_at(2 * u + 3)

    lax.fori_loop(
        0, len(ITEMS) // 2, body, tuple(item_at(jnp.int32(n)) for n in (-1, 0, 1))
    )
    for unit in range(SHARES):
        accumulate(tile_odd, item_at(jnp.int32(len(ITEMS) - 1)), unit)
    send_parts(len(ITEMS) + 2)
    total = sums_of(0, 0)
    own = self_ref[...]
    powers = [own]
    for _ in range(POWERS - 1):
        powers.append(powers[-1] * own)
    total = total + jnp.concatenate(powers, axis=0)
    for n in range(len(PEERS)):
        part_copy(n).wait_recv()
        total = total + incoming[n]
    conn_ref[...] = total
    picked = jnp.concatenate([conn_ref[pl.ds(order_ref[t], 1), :] for t in range(POWERS)], axis=0)
    log_conn = jnp.log(picked)
    results[pl.ds(0, POWERS), :] = log_conn
    out_copies = [pltpu.make_async_copy(results.at[pl.ds(0, POWERS), :], log_conn_ref, out_sem.at[0])]
    out_copies[0].start()

    position = log_conn * ((BINS - 1) / log_total)
    position = jnp.concatenate(
        [position, jnp.zeros((LANES - POWERS, LANES), jnp.float32)], axis=0
    ).T
    levels = lax.broadcasted_iota(jnp.int32, (LANES, BINS), 1).astype(jnp.float32)
    for t in range(POWERS):
        weights = jnp.maximum(0.0, 1.0 - jnp.abs(position[:, t : t + 1] - levels))
        hist_ref[pl.ds(t, 1), :] = jnp.sum(weights, axis=0, keepdims=True)

    here = x * 4 + y

    def hist_copy(n, src):
        dx, dy = PEERS[n]
        return remote(
            hist_ref, plane_hist.at[src], hist_send.at[n], hist_recv.at[n], at(dx=dx, dy=dy)
        )

    for n in range(len(PEERS)):
        hist_copy(n, here).start()
    plane_hist[here] = hist_ref[...]
    for n in range(len(PEERS)):
        dx, dy = PEERS[n]
        hist_copy(n, lax.rem(x + (4 - dx), 4) * 4 + lax.rem(y + (4 - dy), 4)).wait_recv()
    plane_ref[...] = tree_sum([plane_hist[i] for i in range(16)])

    def line_copy(n, src):
        return remote(
            plane_ref, line_hist.at[src], line_send.at[n], line_recv.at[n], at(dz=LINE_PEERS[n])
        )

    for n in range(7):
        line_copy(n, z).start()
    line_hist[z] = plane_ref[...]
    for n in range(7):
        line_copy(n, lax.rem(z + (8 - LINE_PEERS[n]), 8)).wait_recv()
    line_ref[...] = tree_sum([line_hist[i] for i in range(8)])
    last = remote(line_ref, core_hist, last_send, last_recv, at(dc=1))
    last.start()
    last.wait_recv()
    hist = line_ref[...] + core_hist[...]

    hist = jnp.concatenate([hist, jnp.zeros((LANES - POWERS, BINS), jnp.float32)], axis=0).T
    centers = lax.broadcasted_iota(jnp.int32, hist.shape, 0).astype(jnp.float32) * (
        log_total / (BINS - 1)
    )

    def over_bins(value):
        return jnp.sum(value, axis=0, keepdims=True)

    weight_sum = over_bins(hist)
    ylog = jnp.log(hist + 1.0) - log_total
    xdev = centers - over_bins(hist * centers) / weight_sum
    ydev = ylog - over_bins(hist * ylog) / weight_sum
    sxx = jnp.maximum(over_bins(hist * xdev * xdev) / weight_sum, 0.05)
    syy = jnp.maximum(over_bins(hist * ydev * ydev) / weight_sum, 0.05)
    sxy = over_bins(hist * xdev * ydev) / weight_sum
    fit_out[...] = (-sxy * jnp.abs(sxy) / (sxx * syy))[:, :POWERS]
    slope_out[...] = (sxy / sxx)[:, :POWERS]
    out_copies.append(pltpu.make_async_copy(fit_out, fit_ref, out_sem.at[1]))
    out_copies.append(pltpu.make_async_copy(slope_out, slope_ref, out_sem.at[2]))
    for copy in out_copies[1:]:
        copy.start()
    for sends in PLANE_SENDS:
        for send in sends:
            plane_copy(*send).wait_send()
    for step in range(1, Z_STEPS + 1):
        for direction in (1, -1):
            z_copy(direction, step).wait_send()
    for step in range(Z_STEPS + 1):
        core_copy(step).wait_send()
    for n in range(len(PEERS)):
        part_copy(n).wait_send()
        hist_copy(n, here).wait_send()
    for n in range(7):
        line_copy(n, z).wait_send()
    last.wait_send()
    for copy in out_copies:
        copy.wait()


def on_device(expression, power_order):
    genes_dev, samples = expression.shape
    powers = power_order.shape[0]
    total_genes = genes_dev * lax.axis_size(AXES)
    plane, line = len(PEERS), 7
    dma = pltpu.SemaphoreType.DMA
    log_conn, fit, slope = pl.pallas_call(
        functools.partial(kernel, math.log(total_genes), samples),
        out_shape=(
            jax.ShapeDtypeStruct((powers, genes_dev), jnp.float32),
            jax.ShapeDtypeStruct((1, powers), jnp.float32),
            jax.ShapeDtypeStruct((1, powers), jnp.float32),
        ),
        in_specs=[pl.BlockSpec(memory_space=pltpu.HBM), pl.BlockSpec(memory_space=pltpu.SMEM)],
        out_specs=(pl.BlockSpec(memory_space=pltpu.HBM),) * 3,
        scratch_shapes=[
            pltpu.VMEM((SLABS, 2048, LANES), jnp.bfloat16),
            pltpu.VMEM((SLABS, 2048, LANES), jnp.bfloat16),
            pltpu.VMEM((POWERS, 8, 2048), jnp.float32),
            pltpu.VMEM((ROWS + 8 * STEPS, CHUNK), jnp.float32),
            pltpu.VMEM((ROWS + 8 * STEPS, CHUNK), jnp.float32),
            pltpu.VMEM((1, LANES), jnp.float32),
            pltpu.VMEM((plane, powers, LANES), jnp.float32),
            pltpu.VMEM((plane, powers, LANES), jnp.float32),
            pltpu.VMEM((powers, LANES), jnp.float32),
            pltpu.VMEM((powers, BINS), jnp.float32),
            pltpu.VMEM((powers, BINS), jnp.float32),
            pltpu.VMEM((16, powers, BINS), jnp.float32),
            pltpu.VMEM((8, powers, BINS), jnp.float32),
            pltpu.VMEM((powers, BINS), jnp.float32),
            pltpu.VMEM((powers, BINS), jnp.float32),
            pltpu.VMEM((powers, LANES), jnp.float32),
            pltpu.VMEM((1, powers), jnp.float32),
            pltpu.VMEM((1, powers), jnp.float32),
            dma((2, SLABS)),
            dma((4, STEPS)),
            dma((4, STEPS)),
            dma((2, Z_STEPS)),
            dma((2, Z_STEPS)),
            dma((STEPS,)),
            dma((STEPS,)),
            dma((plane,)),
            dma((plane,)),
            dma((plane,)),
            dma((plane,)),
            dma((line,)),
            dma((line,)),
            dma,
            dma,
            dma((3,)),
        ],
        compiler_params=pltpu.CompilerParams(
            collective_id=0, has_side_effects=True, vmem_limit_bytes=66_800_000
        ),
        name="coexpression",
    )(expression, power_order)
    return log_conn.T, fit.reshape(powers), slope.reshape(powers)


def solution(mesh):
    torus = Mesh(mesh.devices.reshape(8, 4, 4, 2), AXES)
    along = P(AXES, None)
    return jax.shard_map(
        on_device,
        mesh=torus,
        in_specs=(along, P()),
        out_specs=(along, P(), P()),
        check_vma=False,
    )
```
